128 devices in a mesh: modes: 16 (over z_lo, y, core), tiles: 8 (over z_hi, x).
Axes of the slice: x: 4, y: 4, z: 4 (z_hi: 2, z_lo: 2; z = z_hi * 2 + z_lo), core: 2. Of those that a mesh axis runs over, the one named last changes fastest.
Arguments:
- solution_modes: float32 [512, 32, 8, 128], P('modes', 'tiles'), may hold values from -6 to 6
- coefficient_modes: float32 [128, 32, 8, 128], P('modes', 'tiles'), may hold values from 0.5 to 4
- coupling: float32 [16, 32, 32, 32], P('modes'), may hold values from -0.03125 to 0.03125
- source_block: int32 [16, 32], P('modes'), may hold values from 0 to 15
- expansion_index: int32 [16, 32], P('modes'), may hold values from 0 to 127
Outputs:
- applied: float32 [512, 32, 8, 128], P('modes', 'tiles')
The draws below stay inside these ranges and needn't reach their ends.
All inputs are finite; a program needn't handle non-finite values.
Results may differ from the reference program's by a relative error of at most 0.0003.
Values sent between devices are 32-bit elements; how exact they have to be, the bound alone decides.
A program may use at most 128 MiB of HBM per device.

```python
import math
import jax
import jax.numpy as jnp
from jax import lax

P_SIZE = 512
K = 128
MB = 32
S = 32
NY = 8
NZ = 128
NBLK = 16
NX = 32


def touch_ends(array, stream_key, least, high):
    longest = array.shape.index(max(array.shape))
    spots = []
    for shift in (0, 1):
        where = [jax.random.randint(jax.random.fold_in(stream_key, axis), (), 0, length) for axis, length in enumerate(array.shape)]
        where[longest] = (where[longest] + shift) % array.shape[longest]
        spots.append(tuple(where))
    return array.at[spots[0]].set(least).at[spots[1]].set(high)


def shard_levels(rng, dims, pieces, low, largest):
    factor_of, own = 1.0, jax.random.fold_in(rng, 6)
    for axis_at, blocks in pieces:
        heights = jnp.exp(jax.random.uniform(jax.random.fold_in(own, axis_at), (blocks,), jnp.float32, low / len(pieces), largest / len(pieces)))
        factor_of = factor_of * jnp.repeat(heights, dims[axis_at] // blocks).reshape([-1 if axis == axis_at else 1 for axis in range(len(dims))])
    return factor_of


def bell_draw(stream_key, dims, spread, limit, split=(), kind=jnp.bfloat16):
    level = shard_levels(stream_key, dims, split, -0.22, 0.18) if split else 1.0
    values = jax.random.normal(stream_key, dims, jnp.float32) * spread * level
    return jnp.minimum(jnp.maximum(values, -limit), limit).astype(kind)


def setup_inputs(seed: int = 0) -> dict:
    streams_of = jax.random.split(jax.random.key(seed), 6)
    return {
        "solution_modes": bell_draw(streams_of[0], (P_SIZE, NX, NY, NZ), 1.0, 6.0, ((0, 16), (1, 8)), jnp.float32),
        "coefficient_modes": jnp.clip(jnp.exp(math.log(4.0) - 2.0794415 * jax.random.uniform(streams_of[1], (K, NX, NY, NZ), jnp.float32) ** shard_levels(streams_of[1], (K, NX, NY, NZ), ((0, 16), (1, 8)), -0.2, 0.2)), 0.5, 4.0),
        "coupling": bell_draw(streams_of[2], (NBLK, S, MB, MB), (40 * S * MB) ** -0.5, 0.03125, ((0, 16),), jnp.float32),
        "source_block": touch_ends(jax.random.randint(streams_of[3], (NBLK, S), 0, NBLK), jax.random.fold_in(streams_of[3], 1), 0, NBLK - 1).astype(jnp.int32),
        "expansion_index": touch_ends(jax.random.randint(streams_of[4], (NBLK, S), 0, K), jax.random.fold_in(streams_of[4], 1), 0, K - 1).astype(jnp.int32),
    }


def face_means(coefficient):
    along_first = 0.5 * (coefficient[:, :-1, 1:-1, 1:-1] + coefficient[:, 1:, 1:-1, 1:-1])
    along_second = 0.5 * (coefficient[:, 1:-1, :-1, 1:-1] + coefficient[:, 1:-1, 1:, 1:-1])
    along_third = 0.5 * (coefficient[:, 1:-1, 1:-1, :-1] + coefficient[:, 1:-1, 1:-1, 1:])
    return along_first, along_second, along_third


def divergence(blended, along_first, along_second, along_third):
    flux_first = along_first * (blended[:, :-1, 1:-1, 1:-1] - blended[:, 1:, 1:-1, 1:-1])
    flux_second = along_second * (blended[:, 1:-1, :-1, 1:-1] - blended[:, 1:-1, 1:, 1:-1])
    flux_third = along_third * (blended[:, 1:-1, 1:-1, :-1] - blended[:, 1:-1, 1:-1, 1:])
    result = flux_first[:, 1:] - flux_first[:, :-1]
    result = result + flux_second[:, :, 1:] - flux_second[:, :, :-1]
    return result + flux_third[:, :, :, 1:] - flux_third[:, :, :, :-1]


def block_output(padded_u, faces, coupling_rows, source_rows, expansion_rows, width):
    first_faces, second_faces, third_faces = faces
    shape = (width, padded_u.shape[1] - 2, padded_u.shape[2] - 2, padded_u.shape[3] - 2)

    def advance(running, slot_index):
        source = source_rows[slot_index].astype(jnp.int32)
        expansion = expansion_rows[slot_index].astype(jnp.int32)
        source_modes = lax.dynamic_slice_in_dim(padded_u, source * width, width, 0)
        block_matrix = coupling_rows[slot_index]
        blended = jnp.einsum("ij,jxyz->ixyz", block_matrix, source_modes, precision=lax.Precision.HIGHEST)
        term = divergence(blended,
                          lax.dynamic_index_in_dim(first_faces, expansion, 0, keepdims=False),
                          lax.dynamic_index_in_dim(second_faces, expansion, 0, keepdims=False),
                          lax.dynamic_index_in_dim(third_faces, expansion, 0, keepdims=False))
        return running + term, None

    start = jnp.zeros(shape, jnp.float32)
    total, _ = lax.scan(advance, start, jnp.arange(source_rows.shape[0], dtype=jnp.int32))
    return total


def reference(solution_modes, coefficient_modes, coupling, source_block, expansion_index):
    padding = ((0, 0), (1, 1), (1, 1), (1, 1))
    padded_u = jnp.pad(solution_modes, padding)
    padded_a = jnp.pad(coefficient_modes, padding)
    faces = face_means(padded_a)

    def one_block(block_index):
        return block_output(padded_u, faces, coupling[block_index], source_block[block_index],
                            expansion_index[block_index], MB)

    stacked = lax.map(one_block, jnp.arange(NBLK, dtype=jnp.int32))
    return stacked.reshape(solution_modes.shape)
```

```python
import functools

import jax
import jax.numpy as jnp
from jax import lax
from jax.experimental import pallas as pl
from jax.experimental.pallas import tpu as pltpu
from jax.sharding import PartitionSpec as P

F32, BF16 = jnp.float32, jnp.bfloat16


def lanes(shape):
    return lax.broadcasted_iota(jnp.int32, shape, len(shape) - 1)


def face_tiles(roll, comb, x0, x1, zh, xm, xp):
    lane = lanes(x0.shape)
    zz, yy, low = lane % 8, (lane // 8) % 8, lane < 64
    zero = jnp.zeros_like(x0)
    r0, r1, rp, rm = (roll(v, 64) for v in (x0, x1, xp, xm))
    fx0 = comb(x0, jnp.where(low, r0, r1))
    fx1 = comb(x1, jnp.where(low, r1, rp))
    fy0 = comb(x0, jnp.where(yy < 7, roll(x0, 120), zero))
    fy1 = comb(x1, jnp.where(yy < 7, roll(x1, 120), zero))
    fz0 = comb(x0, jnp.where(zz < 7, roll(x0, 127), zh))
    fz1 = comb(x1, jnp.where(zz < 7, roll(x1, 127), roll(zh, 1)))
    group = lane // 8
    edge = jnp.where(group == 8, r0, jnp.where(group == 9, roll(x0, 8),
                     jnp.where(group == 10, roll(x1, 80), roll(x1, 24))))
    edge = jnp.where(group < 12, edge, zero)
    t6 = comb(jnp.where(low, rm, zero), jnp.where(low, x0, edge))
    t7 = comb(zh, jnp.where(zz == 0, x0, roll(x1, 1)))
    t7 = jnp.where(zz < 2, t7, zero)
    return fx0, fx1, fy0, fy1, fz0, fz1, t6, t7


def divergence_tiles(roll, fx0, fx1, fy0, fy1, fz0, fz1, t6, t7):
    lane = lanes(fx0.shape)
    zz, yy, low = lane % 8, (lane // 8) % 8, lane < 64
    rx0, rx1 = roll(fx0, 64), roll(fx1, 64)
    ly0 = jnp.where(low, roll(t6, 64), roll(t6, 120))
    ly1 = jnp.where(low, roll(t6, 48), roll(t6, 104))
    out0 = (fx0 - jnp.where(low, t6, rx0)) + (fy0 - jnp.where(yy == 0, ly0, roll(fy0, 8)))
    out0 = out0 + (fz0 - jnp.where(zz == 0, t7, roll(fz0, 1)))
    out1 = (fx1 - jnp.where(low, rx0, rx1)) + (fy1 - jnp.where(yy == 0, ly1, roll(fy1, 8)))
    out1 = out1 + (fz1 - jnp.where(zz == 0, roll(t7, 127), roll(fz1, 1)))
    return out0, out1


def difference(own, other):
    return own - other


def mean(own, other):
    return 0.5 * (own + other)


def xroll(value, shift):
    return jnp.roll(value, shift, axis=-1)


def kroll(value, shift):
    return pltpu.roll(value, shift, value.ndim - 1)


def slots_kernel(sb_ref, ei_ref, c_ref, d_ref, a_ref, out_ref):
    block = pl.program_id(0)
    slots = c_ref.shape[1]
    rows = c_ref.shape[2]
    width = d_ref.shape[2]

    def advance(s, total):
        j = sb_ref[block * slots + s]
        k = ei_ref[block * slots + s]
        v = jnp.dot(c_ref[0, s], d_ref[j], preferred_element_type=F32)
        return total + v.reshape(rows // 8, 8, width) * a_ref[k][None]

    total = lax.fori_loop(0, slots, advance, jnp.zeros((rows // 8, 8, width), F32))
    total = total.reshape(rows, width)
    tiles = [total[:, 128 * t:128 * (t + 1)] for t in range(8)]
    out0, out1 = divergence_tiles(kroll, *tiles)
    out_ref[0, 0] = out0
    out_ref[0, 1] = out1


def slots_call(sb, ei, cext, dext, abar):
    blocks, slots, rows, depth = cext.shape
    return pl.pallas_call(
        slots_kernel,
        out_shape=jax.ShapeDtypeStruct((blocks, 2, rows, 128), F32),
        grid_spec=pltpu.PrefetchScalarGridSpec(
            num_scalar_prefetch=2,
            grid=(blocks,),
            in_specs=[
                pl.BlockSpec((1, slots, rows, depth), lambda b, *_: (b, 0, 0, 0)),
                pl.BlockSpec(memory_space=pltpu.VMEM),
                pl.BlockSpec(memory_space=pltpu.VMEM),
            ],
            out_specs=pl.BlockSpec((1, 2, rows, 128), lambda b, *_: (b, 0, 0, 0)),
        ),
        compiler_params=pltpu.CompilerParams(vmem_limit_bytes=60 << 20),
        name="slots",
    )(sb, ei, cext, dext, abar)


def high_low(value):
    high = lax.reduce_precision(value, 8, 7)
    return high.astype(BF16), (value - high).astype(BF16)


def pieces_of(stacked):
    rows = stacked.shape[0]
    split = stacked.reshape(rows, 2, 2, 8, 16, 8).transpose(4, 1, 0, 2, 3, 5)
    center = split.reshape(16, 2, rows, 128)
    above = jnp.pad(center[1:], ((0, 1), (0, 0), (0, 0), (0, 0)))
    below = jnp.pad(center[:-1], ((1, 0), (0, 0), (0, 0), (0, 0)))
    zz = lanes((16, rows, 128)) % 8
    halo = jnp.where(zz == 7, xroll(above[:, 0], 7), 0.0)
    halo = jnp.where(zz == 6, xroll(above[:, 1], 6), halo)
    halo = jnp.where(zz == 0, xroll(below[:, 0], 121), halo)
    halo = jnp.where(zz == 1, xroll(below[:, 1], 122), halo)
    return jnp.concatenate([center, halo[:, None]], axis=1)


def on_device(solution_modes, coefficient_modes, coupling, source_block, expansion_index):
    nu, na = solution_modes.shape[0], coefficient_modes.shape[0]
    stacked = jnp.concatenate([solution_modes, coefficient_modes], axis=0)
    pieces = pieces_of(stacked)
    got = lax.all_to_all(pieces, "modes", 0, 0, tiled=True)
    tiles = lax.axis_size("tiles")
    up = [(i, i + 1) for i in range(tiles - 1)]
    xm = lax.ppermute(got[:, 1], "tiles", up)
    xp = lax.ppermute(got[:, 0], "tiles", [(j, i) for i, j in up])
    parts = (got[:, 0], got[:, 1], got[:, 2], xm, xp)
    delta = jnp.concatenate(face_tiles(xroll, difference, *(v[:, :nu] for v in parts)), axis=-1)
    abar = jnp.concatenate(face_tiles(xroll, mean, *(v[:, nu:] for v in parts)), axis=-1)
    abar = abar.reshape(16 * na, 1, 1024)
    abar = jnp.broadcast_to(abar, (16 * na, 8, 1024))
    dh, dl = high_low(delta)
    dext = jnp.concatenate([dh, dl, dh], axis=1)
    everyone = lax.all_gather(coupling[0], "modes", axis=0)
    ch, cl = high_low(everyone)
    cext = jnp.concatenate([ch, ch, cl], axis=-1)
    sb = lax.all_gather(source_block[0], "modes", axis=0).reshape(-1)
    ei = lax.all_gather(expansion_index[0], "modes", axis=0).reshape(-1)
    out = slots_call(sb, ei, cext, dext, abar)
    back = lax.all_to_all(out, "modes", 0, 0, tiled=True)
    back = back.reshape(16, 2, nu, 2, 8, 8).transpose(2, 1, 3, 4, 0, 5)
    return back.reshape(solution_modes.shape)


def solution(mesh):
    placed = (
        P("modes", "tiles", None, None),
        P("modes", "tiles", None, None),
        P("modes", None, None, None),
        P("modes", None),
        P("modes", None),
    )
    return jax.shard_map(
        on_device,
        mesh=mesh,
        in_specs=placed,
        out_specs=P("modes", "tiles", None, None),
        check_vma=False,
    )
```

```python
import functools

import jax
import jax.numpy as jnp
from jax import lax
from jax.experimental import pallas as pl
from jax.experimental.pallas import tpu as pltpu
from jax.sharding import PartitionSpec as P

F32, BF16 = jnp.float32, jnp.bfloat16


def lanes(shape):
    return lax.broadcasted_iota(jnp.int32, shape, len(shape) - 1)


def face_tiles(roll, comb, x0, x1, zh, xm, xp):
    lane = lanes(x0.shape)
    zz, yy, low = lane % 8, (lane // 8) % 8, lane < 64
    zero = jnp.zeros_like(x0)
    r0, r1, rp, rm = (roll(v, 64) for v in (x0, x1, xp, xm))
    yield comb(x0, jnp.where(low, r0, r1))
    yield comb(x1, jnp.where(low, r1, rp))
    yield comb(x0, jnp.where(low, rm, r0))
    yield comb(x1, jnp.where(low, r0, r1))
    for x in (x0, x1):
        yield comb(x, jnp.where(yy < 7, roll(x, 120), zero))
    for x in (x0, x1):
        yield comb(x, jnp.where(yy > 0, roll(x, 8), zero))
    yield comb(x0, jnp.where(zz < 7, roll(x0, 127), zh))
    yield comb(x1, jnp.where(zz < 7, roll(x1, 127), roll(zh, 1)))
    yield comb(x0, jnp.where(zz > 0, roll(x0, 1), zh))
    yield comb(x1, jnp.where(zz > 0, roll(x1, 1), roll(zh, 127)))


def difference(own, other):
    return own - other


def mean(own, other):
    return 0.5 * (own + other)


def xroll(value, shift):
    return jnp.roll(value, shift, axis=-1)


def kroll(value, shift):
    return pltpu.roll(value, shift, value.ndim - 1)


def prepare(got_ref, xm_ref, xp_ref, delta, faces, nu):
    def one(j, carry):
        def tiles(rows):
            return (got_ref[j, 0, rows], got_ref[j, 1, rows], got_ref[j, 2, rows], xm_ref[j, rows], xp_ref[j, rows])

        for m in range(nu // 8):
            rows = pl.ds(8 * m, 8)
            for f, value in enumerate(face_tiles(kroll, difference, *tiles(rows))):
                delta[j, f, rows] = value
        own = pl.ds(pl.multiple_of(8 * j, 8), 8)
        for f, value in enumerate(face_tiles(kroll, mean, *tiles(pl.ds(nu, 8)))):
            faces[f, own] = value
        return carry

    lax.fori_loop(0, got_ref.shape[0], one, 0)


def slots_kernel(nu, sb_ref, ei_ref, c_ref, got_ref, xm_ref, xp_ref, out_ref, delta, faces, wh, wl):
    block = pl.program_id(0)

    @pl.when(block == 0)
    def _():
        prepare(got_ref, xm_ref, xp_ref, delta, faces, nu)

    def chunk(c, total):
        for s in range(8):
            j = sb_ref[block * 32 + c * 8 + s]
            k = ei_ref[block * 32 + c * 8 + s]
            for t in range(2):
                coefficient = [faces[2 * f + t, pl.ds(k, 8, stride=0)] for f in range(6)]
                for m in range(nu // 16):
                    pair = []
                    for h in range(2):
                        rows = pl.ds(16 * m + 8 * h, 8)
                        w = coefficient[0] * delta[j, t, rows]
                        for f in range(1, 6):
                            w = w + coefficient[f] * delta[j, 2 * f + t, rows]
                        pair.append(w)
                    w = jnp.concatenate(pair, axis=0)
                    high = w.astype(BF16)
                    place = (pl.ds(nu * s + 16 * m, 16), pl.ds(128 * t, 128))
                    wh[place] = high
                    wl[place] = (w - high.astype(F32)).astype(BF16)
        coupling = c_ref[0, c]
        high = coupling.astype(BF16)
        low = (coupling - high.astype(F32)).astype(BF16)
        both = jnp.dot(jnp.concatenate([high, low], axis=0), wh[...], preferred_element_type=F32)
        return total + (both[:nu] + both[nu:]) + jnp.dot(high, wl[...], preferred_element_type=F32)

    total = lax.fori_loop(0, 4, chunk, jnp.zeros((nu, 256), F32))
    out_ref[0, 0] = total[:, :128]
    out_ref[0, 1] = total[:, 128:]


def slots_call(sb, ei, coupling, got, xm, xp, nu):
    blocks = coupling.shape[0]
    vmem = pl.BlockSpec(memory_space=pltpu.VMEM)
    return pl.pallas_call(
        functools.partial(slots_kernel, nu),
        out_shape=jax.ShapeDtypeStruct((blocks, 2, nu, 128), F32),
        grid_spec=pltpu.PrefetchScalarGridSpec(
            num_scalar_prefetch=2,
            grid=(blocks,),
            in_specs=[pl.BlockSpec((1, 4, nu, 256), lambda b, *_: (b, 0, 0, 0)), vmem, vmem, vmem],
            out_specs=pl.BlockSpec((1, 2, nu, 128), lambda b, *_: (b, 0, 0, 0)),
            scratch_shapes=[
                pltpu.VMEM((16, 12, nu, 128), F32),
                pltpu.VMEM((12, 136, 128), F32),
                pltpu.VMEM((256, 256), BF16),
                pltpu.VMEM((256, 256), BF16),
            ],
        ),
        compiler_params=pltpu.CompilerParams(vmem_limit_bytes=40 << 20),
        name="slots",
    )(sb, ei, coupling, got, xm, xp)


def pieces_of(stacked):
    rows = stacked.shape[0]
    split = stacked.reshape(rows, 2, 2, 8, 16, 8).transpose(4, 1, 0, 2, 3, 5)
    center = split.reshape(16, 2, rows, 128)
    above = jnp.pad(center[1:], ((0, 1), (0, 0), (0, 0), (0, 0)))
    below = jnp.pad(center[:-1], ((1, 0), (0, 0), (0, 0), (0, 0)))
    zz = lanes((16, rows, 128)) % 8
    halo = jnp.where(zz == 7, xroll(above[:, 0], 7), 0.0)
    halo = jnp.where(zz == 6, xroll(above[:, 1], 6), halo)
    halo = jnp.where(zz == 0, xroll(below[:, 0], 121), halo)
    halo = jnp.where(zz == 1, xroll(below[:, 1], 122), halo)
    return jnp.concatenate([center, halo[:, None]], axis=1)


def on_device(solution_modes, coefficient_modes, coupling, source_block, expansion_index):
    nu, na = solution_modes.shape[0], coefficient_modes.shape[0]
    stacked = jnp.concatenate([solution_modes, coefficient_modes], axis=0)
    pieces = pieces_of(stacked)
    got = lax.all_to_all(pieces, "modes", 0, 0, tiled=True)
    tiles = lax.axis_size("tiles")
    up = [(i, i + 1) for i in range(tiles - 1)]
    xm = lax.ppermute(got[:, 1], "tiles", up)
    xp = lax.ppermute(got[:, 0], "tiles", [(j, i) for i, j in up])
    packed = coupling[0].reshape(4, 8, nu, nu).transpose(0, 2, 1, 3).reshape(4, nu, 8 * nu)
    packed = lax.all_gather(packed, "modes", axis=0)
    sb = lax.all_gather(source_block[0], "modes", axis=0).reshape(-1)
    ei = lax.all_gather(expansion_index[0], "modes", axis=0).reshape(-1)
    out = slots_call(sb, ei, packed, got, xm, xp, nu)
    back = lax.all_to_all(out, "modes", 0, 0, tiled=True)
    back = back.reshape(16, 2, nu, 2, 8, 8).transpose(2, 1, 3, 4, 0, 5)
    return back.reshape(solution_modes.shape)


def solution(mesh):
    placed = (
        P("modes", "tiles", None, None),
        P("modes", "tiles", None, None),
        P("modes", None, None, None),
        P("modes", None),
        P("modes", None),
    )
    return jax.shard_map(
        on_device,
        mesh=mesh,
        in_specs=placed,
        out_specs=P("modes", "tiles", None, None),
        check_vma=False,
    )
```

```python
import functools

import jax
import jax.numpy as jnp
from jax import lax
from jax.experimental import pallas as pl
from jax.experimental.pallas import tpu as pltpu
from jax.sharding import PartitionSpec as P

F32, BF16 = jnp.float32, jnp.bfloat16


def lanes(shape):
    return lax.broadcasted_iota(jnp.int32, shape, len(shape) - 1)


def face_tiles(roll, comb, x0, x1, zh, xm, xp):
    lane = lanes(x0.shape)
    zz, yy, low = lane % 8, (lane // 8) % 8, lane < 64
    zero = jnp.zeros_like(x0)
    r0, r1, rp, rm = (roll(v, 64) for v in (x0, x1, xp, xm))
    yield comb(x0, jnp.where(low, r0, r1))
    yield comb(x1, jnp.where(low, r1, rp))
    yield comb(x0, jnp.where(low, rm, r0))
    yield comb(x1, jnp.where(low, r0, r1))
    for x in (x0, x1):
        yield comb(x, jnp.where(yy < 7, roll(x, 120), zero))
    for x in (x0, x1):
        yield comb(x, jnp.where(yy > 0, roll(x, 8), zero))
    yield comb(x0, jnp.where(zz < 7, roll(x0, 127), zh))
    yield comb(x1, jnp.where(zz < 7, roll(x1, 127), roll(zh, 1)))
    yield comb(x0, jnp.where(zz > 0, roll(x0, 1), zh))
    yield comb(x1, jnp.where(zz > 0, roll(x1, 1), roll(zh, 127)))


def difference(own, other):
    return own - other


def mean(own, other):
    return 0.5 * (own + other)


def kroll(value, shift):
    return pltpu.roll(value, shift, value.ndim - 1)


def prepare(got_ref, xm_ref, xp_ref, delta, faces, nu):
    def one(j, carry):
        def tiles(rows):
            return (got_ref[j, 0, rows], got_ref[j, 1, rows], got_ref[j, 2, rows], xm_ref[j, rows], xp_ref[j, rows])

        for m in range(nu // 8):
            rows = pl.ds(8 * m, 8)
            for f, value in enumerate(face_tiles(kroll, difference, *tiles(rows))):
                delta[j, f, rows] = value
        own = pl.ds(pl.multiple_of(8 * j, 8), 8)
        for f, value in enumerate(face_tiles(kroll, mean, *tiles(pl.ds(nu, 8)))):
            faces[f, own] = value
        return carry

    lax.fori_loop(0, got_ref.shape[0], one, 0)


def slots_kernel(nu, sb_ref, ei_ref, c_ref, got_ref, xm_ref, xp_ref, out_ref, delta, faces, wh, wl):
    block = pl.program_id(0)

    @pl.when(block == 0)
    def _():
        prepare(got_ref, xm_ref, xp_ref, delta, faces, nu)

    def chunk(c, total):
        for s in range(8):
            j = sb_ref[block * 32 + c * 8 + s]
            k = ei_ref[block * 32 + c * 8 + s]
            for t in range(2):
                coefficient = [faces[2 * f + t, pl.ds(k, 8, stride=0)] for f in range(6)]
                for m in range(nu // 16):
                    pair = []
                    for h in range(2):
                        rows = pl.ds(16 * m + 8 * h, 8)
                        w = coefficient[0] * delta[j, t, rows]
                        for f in range(1, 6):
                            w = w + coefficient[f] * delta[j, 2 * f + t, rows]
                        pair.append(w)
                    w = jnp.concatenate(pair, axis=0)
                    high = w.astype(BF16)
                    place = (pl.ds(nu * s + 16 * m, 16), pl.ds(128 * t, 128))
                    wh[place] = high
                    wl[place] = (w - high.astype(F32)).astype(BF16)
        coupling = c_ref[0, pl.ds(pl.multiple_of(nu * c, nu), nu)]
        high = coupling.astype(BF16)
        low = (coupling - high.astype(F32)).astype(BF16)
        both = jnp.dot(jnp.concatenate([high, low], axis=0), wh[...], preferred_element_type=F32)
        return total + (both[:nu] + both[nu:]) + jnp.dot(high, wl[...], preferred_element_type=F32)

    total = lax.fori_loop(0, 4, chunk, jnp.zeros((nu, 256), F32))
    out_ref[0, 0] = total[:, :128]
    out_ref[0, 1] = total[:, 128:]


def slots_call(sb, ei, coupling, got, xm, xp, nu):
    blocks = coupling.shape[0]
    vmem = pl.BlockSpec(memory_space=pltpu.VMEM)
    return pl.pallas_call(
        functools.partial(slots_kernel, nu),
        out_shape=jax.ShapeDtypeStruct((blocks, 2, nu, 128), F32),
        grid_spec=pltpu.PrefetchScalarGridSpec(
            num_scalar_prefetch=2,
            grid=(blocks,),
            in_specs=[pl.BlockSpec((1, 4 * nu + 8, 256), lambda b, *_: (b, 0, 0)), vmem, vmem, vmem],
            out_specs=pl.BlockSpec((1, 2, nu, 128), lambda b, *_: (b, 0, 0, 0)),
            scratch_shapes=[
                pltpu.VMEM((16, 12, nu, 128), F32),
                pltpu.VMEM((12, 136, 128), F32),
                pltpu.VMEM((256, 256), BF16),
                pltpu.VMEM((256, 256), BF16),
            ],
        ),
        compiler_params=pltpu.CompilerParams(vmem_limit_bytes=40 << 20),
        name="slots",
    )(sb, ei, coupling, got, xm, xp)


def transpose_blocks(rows):
    lane = lanes(rows[0].shape)
    for d in (1, 2, 4, 8):
        keep = (lane // 8) & d == 0
        fresh = list(rows)
        for i in range(16):
            if not i & d:
                fresh[i] = jnp.where(keep, rows[i], kroll(rows[i + d], 8 * d))
                fresh[i + d] = jnp.where(keep, kroll(rows[i], 128 - 8 * d), rows[i + d])
        rows = fresh
    return rows


def cut(value_ref, pieces, count, first):
    def one(m, carry):
        place = pl.ds(pl.multiple_of(first + 8 * m, 8), 8)
        for t in range(2):
            rows = [value_ref[pl.ds(256 * m + 16 * t + i, 8, stride=32), :] for i in range(16)]
            for p, value in enumerate(transpose_blocks(rows)):
                pieces[p + 1, t, place] = value
        return carry

    lax.fori_loop(0, count // 8, one, 0)


def rims(pieces):
    rows = pieces.shape[2]
    for t in range(2):
        pieces[0, t] = jnp.zeros((rows, 128), F32)
        pieces[17, t] = jnp.zeros((rows, 128), F32)

    def one(p, carry):
        for m in range(rows // 8):
            place = pl.ds(8 * m, 8)
            zz = lanes((8, 128)) % 8
            rim = jnp.where(zz == 7, kroll(pieces[p + 2, 0, place], 7), 0.0)
            rim = jnp.where(zz == 6, kroll(pieces[p + 2, 1, place], 6), rim)
            rim = jnp.where(zz == 0, kroll(pieces[p, 0, place], 121), rim)
            rim = jnp.where(zz == 1, kroll(pieces[p, 1, place], 122), rim)
            pieces[p + 1, 2, place] = rim
        return carry

    lax.fori_loop(0, 16, one, 0)


def pack(c_ref, index_ref, held, me):
    n = c_ref.shape[1]
    for q in range(4):
        for h in range(2):
            for m in range(n // 8):
                parts = [c_ref[8 * q + 4 * h + l, pl.ds(8 * m, 8), :] for l in range(4)]
                held[me, pl.ds(n * q + 8 * m, 8), pl.ds(128 * h, 128)] = jnp.concatenate(parts, axis=1)
    held[me, pl.ds(4 * n, 8), :] = index_ref[...]


def remote(src, dst, send, recv, **where):
    return pltpu.make_async_remote_copy(
        src_ref=src, dst_ref=dst, send_sem=send, recv_sem=recv,
        device_id=where, device_id_type=pl.DeviceIdType.MESH)


def greet(others):
    barrier = pltpu.get_barrier_semaphore()
    for where in others:
        pl.semaphore_signal(barrier, inc=1, device_id=where, device_id_type=pl.DeviceIdType.MESH)
    return barrier


def spread_kernel(u_ref, a_ref, c_ref, index_ref, got, xm, xp, held, pieces,
                  p_send, p_recv, m_send, m_recv, q_send, q_recv, c_send, c_recv, own_sem):
    me, tile = lax.axis_index("modes"), lax.axis_index("tiles")
    tiles = lax.axis_size("tiles")
    has_up, has_down = tile < tiles - 1, tile > 0
    peers = [lax.rem(me + d, 16) for d in range(1, 16)]
    z, y, core = me // 8, lax.rem(me // 2, 4), lax.rem(me, 2)

    def block(dz, dy, dc):
        return lax.rem(z + dz, 2) * 8 + lax.rem(y + dy, 4) * 2 + lax.rem(core + dc, 2)

    across = {"modes": block(1, 0, 0), "tiles": lax.rem(tile + tiles // 2, tiles)}
    barrier = greet([{"modes": p} for p in peers] + [across])

    @pl.when(has_up)
    def _():
        pl.semaphore_signal(barrier, inc=1, device_id={"tiles": tile + 1}, device_id_type=pl.DeviceIdType.MESH)

    @pl.when(has_down)
    def _():
        pl.semaphore_signal(barrier, inc=1, device_id={"tiles": tile - 1}, device_id_type=pl.DeviceIdType.MESH)

    nu, na = u_ref.shape[0] // 32, a_ref.shape[0] // 32
    cut(u_ref, pieces, nu, 0)
    cut(a_ref, pieces, na, nu)
    rims(pieces)
    pack(c_ref, index_ref, held, me)
    zero = jnp.zeros(xm.shape[1:], F32)

    @pl.when(jnp.logical_not(has_down))
    def _():
        for j in range(16):
            xm[j] = zero

    @pl.when(jnp.logical_not(has_up))
    def _():
        for j in range(16):
            xp[j] = zero

    pl.semaphore_wait(barrier, 16 + has_up.astype(jnp.int32) + has_down.astype(jnp.int32))
    own = pltpu.make_async_copy(pieces.at[me + 1], got.at[me], own_sem)
    own.start()
    out = [remote(pieces.at[p + 1], got.at[me], p_send.at[i], p_recv.at[me], modes=p) for i, p in enumerate(peers)]
    for copy in out:
        copy.start()

    def share(i, which, **where):
        copy = remote(held.at[which], held.at[which], c_send.at[i], c_recv.at[which], **where)
        copy.start()
        return copy

    def landed(which):
        remote(held.at[which], held.at[which], c_send.at[0], c_recv.at[which], modes=block(0, 0, 1)).wait_recv()

    sent = [share(i, me, modes=block(0, dy, 0)) for i, dy in enumerate((1, 3, 2))]
    sent.append(share(3, me, modes=block(1, 0, 0)))
    sent.append(share(4, me, modes=block(0, 0, 1)))

    def upward(j):
        return remote(got.at[j, 1], xm.at[j], m_send.at[j], m_recv.at[j], tiles=tile + 1)

    def downward(j):
        return remote(got.at[j, 0], xp.at[j], q_send.at[j], q_recv.at[j], tiles=tile - 1)

    def forward(j):
        @pl.when(has_up)
        def _():
            upward(j).start()

        @pl.when(has_down)
        def _():
            downward(j).start()

    own.wait()
    forward(me)
    for d in range(1, 16):
        source = lax.rem(me + 16 - d, 16)
        remote(pieces.at[1], got.at[source], p_send.at[0], p_recv.at[source], modes=peers[0]).wait_recv()
        forward(source)

    for i, dy in enumerate((1, 3, 2)):
        which = block(0, dy, 0)
        landed(which)
        sent.append(share(5 + 2 * i, which, modes=block(0, 0, 1)))
        where = {"modes": block(1, 0, 0)} if dy == 1 else across
        sent.append(share(6 + 2 * i, which, **where))
    for dy in range(4):
        which = block(1, dy, 0)
        landed(which)
        sent.append(share(11 + dy, which, modes=block(0, 0, 1)))
    for dz in range(2):
        for dy in range(4):
            landed(block(dz, dy, 1))
    for copy in sent + out:
        copy.wait_send()

    def finish(j, carry):
        @pl.when(has_up)
        def _():
            upward(j).wait_send()
            remote(got.at[j, 0], xp.at[j], q_send.at[j], q_recv.at[j], tiles=tile + 1).wait_recv()

        @pl.when(has_down)
        def _():
            downward(j).wait_send()
            remote(got.at[j, 1], xm.at[j], m_send.at[j], m_recv.at[j], tiles=tile - 1).wait_recv()

        return carry

    lax.fori_loop(0, 16, finish, 0)


def spread(u, a, coupling, index):
    rows = (u.shape[0] + a.shape[0]) // 32
    n = coupling.shape[1]
    vmem = pl.BlockSpec(memory_space=pltpu.VMEM)
    dma = pltpu.SemaphoreType.DMA
    return pl.pallas_call(
        spread_kernel,
        out_shape=(
            jax.ShapeDtypeStruct((16, 3, rows, 128), F32),
            jax.ShapeDtypeStruct((16, rows, 128), F32),
            jax.ShapeDtypeStruct((16, rows, 128), F32),
            jax.ShapeDtypeStruct((16, 4 * n + 8, 256), F32),
        ),
        in_specs=[vmem] * 4,
        out_specs=(vmem,) * 4,
        scratch_shapes=[
            pltpu.VMEM((18, 3, rows, 128), F32),
            dma((15,)), dma((16,)), dma((16,)), dma((16,)), dma((16,)), dma((16,)), dma((15,)), dma((16,)), dma,
        ],
        compiler_params=pltpu.CompilerParams(collective_id=0, has_side_effects=True, vmem_limit_bytes=40 << 20),
        name="spread",
    )(u, a, coupling, index)


def gather_kernel(part_ref, out_ref, back, send, recv, own_sem):
    me = lax.axis_index("modes")
    peers = [lax.rem(me + d, 16) for d in range(1, 16)]
    barrier = greet([{"modes": p} for p in peers])
    pl.semaphore_wait(barrier, 15)
    own = pltpu.make_async_copy(part_ref.at[me], back.at[me], own_sem)
    own.start()
    out = [remote(part_ref.at[p], back.at[me], send.at[i], recv.at[me], modes=p) for i, p in enumerate(peers)]
    for copy in out:
        copy.start()
    own.wait()
    for d in range(1, 16):
        source = lax.rem(me + 16 - d, 16)
        remote(part_ref.at[0], back.at[source], send.at[0], recv.at[source], modes=peers[0]).wait_recv()

    def one(m, carry):
        place = pl.ds(pl.multiple_of(8 * m, 8), 8)
        for t in range(2):
            rows = [back[p, t, place] for p in range(16)]
            for i, value in enumerate(transpose_blocks(rows)):
                out_ref[pl.ds(256 * m + 16 * t + i, 8, stride=32), :] = value
        return carry

    lax.fori_loop(0, part_ref.shape[2] // 8, one, 0)
    for copy in out:
        copy.wait_send()


def gather(part):
    vmem = pl.BlockSpec(memory_space=pltpu.VMEM)
    dma = pltpu.SemaphoreType.DMA
    return pl.pallas_call(
        gather_kernel,
        out_shape=jax.ShapeDtypeStruct((part.shape[2] * 32, 128), F32),
        in_specs=[vmem],
        out_specs=vmem,
        scratch_shapes=[pltpu.VMEM(part.shape, F32), dma((15,)), dma((16,)), dma],
        compiler_params=pltpu.CompilerParams(collective_id=1, has_side_effects=True, vmem_limit_bytes=40 << 20),
        name="gather",
    )(part)


def on_device(solution_modes, coefficient_modes, coupling, source_block, expansion_index):
    nu = solution_modes.shape[0]
    slots = source_block.shape[1]
    index = jnp.concatenate([source_block, expansion_index], axis=1).astype(F32)
    index = jnp.pad(index, ((0, 7), (0, 256 - 2 * slots)))
    got, xm, xp, held = spread(
        solution_modes.reshape(-1, 128), coefficient_modes.reshape(-1, 128), coupling[0], index)
    index = held[:, 4 * nu, :2 * slots].astype(jnp.int32)
    sb, ei = index[:, :slots].reshape(-1), index[:, slots:].reshape(-1)
    out = slots_call(sb, ei, held, got, xm, xp, nu)
    return gather(out).reshape(solution_modes.shape)


def solution(mesh):
    placed = (
        P("modes", "tiles", None, None),
        P("modes", "tiles", None, None),
        P("modes", None, None, None),
        P("modes", None),
        P("modes", None),
    )
    return jax.shard_map(
        on_device,
        mesh=mesh,
        in_specs=placed,
        out_specs=P("modes", "tiles", None, None),
        check_vma=False,
    )
```

```python
import functools

import jax
import jax.numpy as jnp
from jax import lax
from jax.experimental import pallas as pl
from jax.experimental.pallas import tpu as pltpu
from jax.sharding import PartitionSpec as P

F32, BF16 = jnp.float32, jnp.bfloat16


def lanes(shape):
    return lax.broadcasted_iota(jnp.int32, shape, len(shape) - 1)


def difference(own, other):
    return own - other


def mean(own, other):
    return 0.5 * (own + other)


def kroll(value, shift):
    return pltpu.roll(value, shift, value.ndim - 1)


def transpose_blocks(rows):
    lane = lanes(rows[0].shape)
    for d in (1, 2, 4, 8):
        keep = (lane // 8) & d == 0
        fresh = list(rows)
        for i in range(16):
            if not i & d:
                fresh[i] = jnp.where(keep, rows[i], kroll(rows[i + d], 8 * d))
                fresh[i + d] = jnp.where(keep, kroll(rows[i], 128 - 8 * d), rows[i + d])
        rows = fresh
    return rows


def remote(src, dst, send, recv, **where):
    return pltpu.make_async_remote_copy(
        src_ref=src, dst_ref=dst, send_sem=send, recv_sem=recv,
        device_id=where, device_id_type=pl.DeviceIdType.MESH)


def greet(others):
    barrier = pltpu.get_barrier_semaphore()
    for where in others:
        pl.semaphore_signal(barrier, inc=1, device_id=where, device_id_type=pl.DeviceIdType.MESH)
    return barrier


def face_tiles(comb, x0, x1, below, above, r_minus, r_plus):
    lane = lanes(x0.shape)
    zz, yy, low = lane % 8, (lane // 8) % 8, lane < 64
    zero = jnp.zeros_like(x0)
    r0, r1 = kroll(x0, 64), kroll(x1, 64)
    yield comb(x0, jnp.where(low, r0, r1))
    yield comb(x1, jnp.where(low, r1, r_plus))
    yield comb(x0, jnp.where(low, r_minus, r0))
    yield comb(x1, jnp.where(low, r0, r1))
    for x in (x0, x1):
        yield comb(x, jnp.where(yy < 7, kroll(x, 120), zero))
    for x in (x0, x1):
        yield comb(x, jnp.where(yy > 0, kroll(x, 8), zero))
    for x, rim in zip((x0, x1), above):
        yield comb(x, jnp.where(zz < 7, kroll(x, 127), rim))
    for x, rim in zip((x0, x1), below):
        yield comb(x, jnp.where(zz > 0, kroll(x, 1), rim))


def cut(value_ref, pieces, count, first, span):
    def one(m, carry):
        for t in range(2):
            place = pl.ds(pl.multiple_of(span * t + first + 8 * m, 8), 8)
            rows = [value_ref[pl.ds(256 * m + 16 * t + i, 8, stride=32), :] for i in range(16)]
            for p, value in enumerate(transpose_blocks(rows)):
                pieces[p + 1, place] = value
        return carry

    lax.fori_loop(0, count // 8, one, 0)


def rims(pieces, nu, na):
    span = nu + na
    for q in (0, 17):
        pieces[q, pl.ds(0, 2 * span)] = jnp.zeros((2 * span, 128), F32)

    def one(p, carry):
        zz = lanes((8, 128)) % 8

        def rim(first, spots, base):
            for (t, side), spot in spots:
                value = pieces[p + 2 * side, pl.ds(span * t + first, 8)]
                shift = (spot - (0 if side else 7)) % 128
                base = jnp.where(zz == spot, kroll(value, shift), base)
            return base

        outer = (((0, 1), 7), ((1, 1), 6), ((0, 0), 0), ((1, 0), 1))
        inner = (((0, 1), 5), ((1, 1), 4), ((0, 0), 2), ((1, 0), 3))
        for m in range(nu // 16):
            value = rim(8 * m, outer, jnp.zeros((8, 128), F32))
            pieces[p + 1, pl.ds(2 * span + 8 * m, 8)] = rim(nu // 2 + 8 * m, inner, value)
        for m in range(na // 8):
            pieces[p + 1, pl.ds(2 * span + nu // 2 + 8 * m, 8)] = rim(nu + 8 * m, outer, jnp.zeros((8, 128), F32))
        return carry

    lax.fori_loop(0, 16, one, 0, unroll=2)


def pack(c_ref, held, me):
    n = c_ref.shape[1]
    for q in range(4):
        for h in range(2):
            for m in range(n // 8):
                parts = [c_ref[8 * q + 4 * h + l, pl.ds(8 * m, 8), :] for l in range(4)]
                held[me, pl.ds(n * q + 8 * m, 8), pl.ds(128 * h, 128)] = jnp.concatenate(parts, axis=1)


def kernel(u_hbm, a_hbm, c_hbm, sb_ref, ei_ref, out_ref,
           u_ref, a_ref, c_ref, pieces, got, up_out, down_out, from_down, from_up, held, part, back,
           delta, faces, wh, wl, index_v, index_s,
           in_sem, p_send, p_recv, m_send, m_recv, q_send, q_recv, c_send, c_recv, o_send, o_recv, i_send, i_recv, own_sem):
    me, tile = lax.axis_index("modes"), lax.axis_index("tiles")
    tiles = lax.axis_size("tiles")
    has_up, has_down = tile < tiles - 1, tile > 0
    z, y, core = me // 8, lax.rem(me // 2, 4), lax.rem(me, 2)
    nu, na = u_ref.shape[0] // 32, a_ref.shape[0] // 32
    span = nu + na
    slots = c_ref.shape[0]

    def block(dz, dy, dc):
        return lax.rem(z + dz, 2) * 8 + lax.rem(y + dy, 4) * 2 + lax.rem(core + dc, 2)

    loads = [pltpu.make_async_copy(s, d, in_sem.at[i])
             for i, (s, d) in enumerate(((u_hbm, u_ref), (a_hbm, a_ref), (c_hbm, c_ref)))]
    for load in loads:
        load.start()
    opposite = lax.rem(tile + tiles // 2, tiles)
    chips = ((0, 0), (0, 1), (0, 3), (1, 0), (0, 2), (1, 1), (1, 3), (1, 2))
    offsets = [(dz, dy, dc) for dz, dy in chips for dc in range(2)][1:]
    barrier = greet([{"modes": block(*o)} for o in offsets] + [{"modes": block(1, 0, 0), "tiles": opposite}])

    @pl.when(has_up)
    def _():
        pl.semaphore_signal(barrier, inc=1, device_id={"tiles": tile + 1}, device_id_type=pl.DeviceIdType.MESH)

    @pl.when(has_down)
    def _():
        pl.semaphore_signal(barrier, inc=1, device_id={"tiles": tile - 1}, device_id_type=pl.DeviceIdType.MESH)

    loads[0].wait()
    cut(u_ref, pieces, nu, 0, span)
    loads[1].wait()
    cut(a_ref, pieces, na, nu, span)
    rims(pieces, nu, na)
    index_v[me] = jnp.zeros((8, 128), jnp.int32)
    index_v[me, pl.ds(0, 1), pl.ds(0, slots)] = sb_ref[...]
    index_v[me, pl.ds(1, 1), pl.ds(0, slots)] = ei_ref[...]

    @pl.when(jnp.logical_not(has_down))
    def _():
        from_down[...] = jnp.zeros(from_down.shape, F32)

    @pl.when(jnp.logical_not(has_up))
    def _():
        from_up[...] = jnp.zeros(from_up.shape, F32)

    pl.semaphore_wait(barrier, 16 + has_up.astype(jnp.int32) + has_down.astype(jnp.int32))

    own = pltpu.make_async_copy(pieces.at[me + 1], got.at[me], own_sem)
    own.start()
    sends = []
    for i, o in enumerate(offsets):
        copy = remote(pieces.at[block(*o) + 1], got.at[me], p_send.at[i], p_recv.at[me], modes=block(*o))
        copy.start()
        sends.append(copy)
    for i, o in enumerate(offsets):
        copy = remote(index_v.at[me], index_v.at[me], i_send.at[i], i_recv.at[me], modes=block(*o))
        copy.start()
        sends.append(copy)
    loads[2].wait()
    pack(c_ref, held, me)

    def upward(g):
        return remote(up_out.at[g], from_down.at[g], m_send.at[g], m_recv.at[g], tiles=tile + 1)

    def downward(g):
        return remote(down_out.at[g], from_up.at[g], q_send.at[g], q_recv.at[g], tiles=tile - 1)

    low = lanes((8, 128)) < 64
    own.wait()
    for dz, dy in chips:
        for dc in range(2):
            if (dz, dy, dc) != (0, 0, 0):
                source = block(dz, dy, dc)
                remote(pieces.at[1], got.at[source], p_send.at[0], p_recv.at[source], modes=source).wait_recv()
        g = block(dz, dy, 0) // 2
        for m in range(span // 8):
            first = pl.ds(8 * m, 8)
            second = pl.ds(span + 8 * m, 8)
            up_out[g, first] = jnp.where(low, kroll(got[2 * g, second], 64), got[2 * g + 1, second])
            down_out[g, first] = jnp.where(low, got[2 * g, first], kroll(got[2 * g + 1, first], 64))

        @pl.when(has_up)
        def _():
            upward(g).start()

        @pl.when(has_down)
        def _():
            downward(g).start()

    def share(i, which, modes, to):
        return remote(held.at[which], held.at[which], c_send.at[i], c_recv.at[which], modes=modes, tiles=to)

    for i, dy in enumerate((1, 3, 2)):
        share(i, me, block(0, dy, 0), tile).start()
    share(3, me, block(1, 0, 0), tile).start()
    share(4, me, block(0, 0, 1), tile).start()
    for o in offsets:
        source = block(*o)
        remote(index_v.at[source], index_v.at[source], i_send.at[0], i_recv.at[source], modes=source).wait_recv()
    indices = pltpu.make_async_copy(index_v, index_s, own_sem)
    indices.start()

    def prepare(i, carry):
        dz, r = i // 4, i % 4
        g = block(dz, r + (r // 2) * (1 - 2 * (r % 2)), 0) // 2

        @pl.when(has_up)
        def _():
            remote(down_out.at[g], from_up.at[g], q_send.at[g], q_recv.at[g], tiles=tile + 1).wait_recv()

        @pl.when(has_down)
        def _():
            remote(up_out.at[g], from_down.at[g], m_send.at[g], m_recv.at[g], tiles=tile - 1).wait_recv()

        for odd in range(2):
            j = 2 * g + odd

            def tiles_of(first, rim, shifts):
                minus, plus = from_down[g, pl.ds(first, 8)], from_up[g, pl.ds(first, 8)]
                minus, plus = (kroll(minus, 64), plus) if odd else (minus, kroll(plus, 64))
                value = got[j, pl.ds(2 * span + rim, 8)]
                below = [kroll(value, s % 128) if s else value for s in shifts[:2]]
                above = [kroll(value, s % 128) if s else value for s in shifts[2:]]
                return got[j, pl.ds(first, 8)], got[j, pl.ds(span + first, 8)], below, above, minus, plus

            for m in range(nu // 8):
                lower = m < nu // 16
                rim = 8 * m if lower else 8 * m - nu // 2
                parts = tiles_of(8 * m, rim, (0, -1, 0, 1) if lower else (-2, -3, 2, 3))
                for f, value in enumerate(face_tiles(difference, *parts)):
                    delta[j, f, pl.ds(8 * m, 8)] = value
            place = pl.ds(pl.multiple_of(8 * j, 8), 8)
            for f, value in enumerate(face_tiles(mean, *tiles_of(nu, nu // 2, (0, -1, 0, 1)))):
                faces[f, place] = value
        return carry

    lax.fori_loop(0, 8, prepare, 0)
    indices.wait()

    def build(b, c, buffer):
        for s in range(8):
            slot = c * 8 + s
            j = index_s[b, 0, slot]
            k = index_s[b, 1, slot]
            for t in range(2):
                coefficient = [faces[2 * f + t, pl.ds(k, 8, stride=0)] for f in range(6)]
                for m in range(nu // 16):
                    pair = []
                    for h in range(2):
                        rows = pl.ds(16 * m + 8 * h, 8)
                        w = coefficient[0] * delta[j, t, rows]
                        for f in range(1, 6):
                            w = w + coefficient[f] * delta[j, 2 * f + t, rows]
                        pair.append(w)
                    w = jnp.concatenate(pair, axis=0)
                    high = w.astype(BF16)
                    place = (buffer, pl.ds(nu * s + 16 * m, 16), pl.ds(128 * t, 128))
                    wh[place] = high
                    wl[place] = (w - high.astype(F32)).astype(BF16)

    def product(b, c, buffer):
        coupling = held[b, pl.ds(nu * c, nu)]
        high = coupling.astype(BF16)
        small = (coupling - high.astype(F32)).astype(BF16)
        both = jnp.dot(jnp.concatenate([high, small], axis=0), wh[buffer], preferred_element_type=F32)
        return (both[:nu] + both[nu:]) + jnp.dot(high, wl[buffer], preferred_element_type=F32)

    def number(i):
        k = i // 2
        r = k % 4
        return k // 4, r + (r // 2) * (1 - 2 * (r % 2)), i % 2

    def deliver(i):
        b = block(*number(i))
        return remote(part.at[b], back.at[me], o_send.at[i - 1], o_recv.at[me], modes=b)

    def advance(i, carry):
        dz, dy, dc = number(i)
        b = block(dz, dy, dc)

        @pl.when(i > 0)
        def _():
            share(0, b, block(0, 0, 1), tile).wait_recv()

        @pl.when(jnp.logical_and(i > 1, dc == 0))
        def _():
            share(4 + i // 2, b, block(0, 0, 1), tile).start()

        @pl.when(jnp.logical_and(jnp.logical_and(i > 1, dc == 0), dz == 0))
        def _():
            share(11 + i // 2, b, block(1, 0, 0), lax.rem(tile + (dy // 2) * (tiles // 2), tiles)).start()

        total = None
        for c in range(slots // 8):
            build(b, c, c % 2)
            term = product(b, c, c % 2)
            total = term if total is None else total + term

        part[b, 0] = total[:, :128]
        part[b, 1] = total[:, 128:]

        @pl.when(i == 0)
        def _():
            back[me, 0] = total[:, :128]
            back[me, 1] = total[:, 128:]

        @pl.when(i > 1)
        def _():
            deliver(i - 1).start()

        return carry

    lax.fori_loop(0, 16, advance, 0)
    deliver(15).start()

    for dz, dy, dc in offsets:
        source = block(dz, dy, dc)
        remote(part.at[0], back.at[source], o_send.at[0], o_recv.at[source], modes=source).wait_recv()

    def restore(m, carry):
        place = pl.ds(pl.multiple_of(8 * m, 8), 8)
        for t in range(2):
            rows = [back[p, t, place] for p in range(16)]
            for i, value in enumerate(transpose_blocks(rows)):
                out_ref[pl.ds(256 * m + 16 * t + i, 8, stride=32), :] = value
        return carry

    lax.fori_loop(0, nu // 8, restore, 0)
    for copy in sends:
        copy.wait_send()
    for i in range(15):
        share(i, me, block(0, 0, 1), tile).wait_send()
        deliver(i + 1).wait_send()
    for g in range(8):
        @pl.when(has_up)
        def _():
            upward(g).wait_send()

        @pl.when(has_down)
        def _():
            downward(g).wait_send()


def on_device(solution_modes, coefficient_modes, coupling, source_block, expansion_index):
    nu, na = solution_modes.shape[0], coefficient_modes.shape[0]
    span, slots = nu + na, source_block.shape[1]
    rows = 2 * span + nu // 2 + na
    vmem = pl.BlockSpec(memory_space=pltpu.VMEM)
    hbm = pl.BlockSpec(memory_space=pl.ANY)
    dma = pltpu.SemaphoreType.DMA
    out = pl.pallas_call(
        kernel,
        out_shape=jax.ShapeDtypeStruct((nu * 32, 128), F32),
        in_specs=[hbm, hbm, hbm, vmem, vmem],
        out_specs=vmem,
        scratch_shapes=[
            pltpu.VMEM((nu * 32, 128), F32), pltpu.VMEM((na * 32, 128), F32), pltpu.VMEM((slots, nu, nu), F32),
            pltpu.VMEM((18, rows, 128), F32), pltpu.VMEM((16, rows, 128), F32),
            pltpu.VMEM((8, span, 128), F32), pltpu.VMEM((8, span, 128), F32),
            pltpu.VMEM((8, span, 128), F32), pltpu.VMEM((8, span, 128), F32),
            pltpu.VMEM((16, slots // 8 * nu, 256), F32),
            pltpu.VMEM((16, 2, nu, 128), F32), pltpu.VMEM((16, 2, nu, 128), F32),
            pltpu.VMEM((16, 12, nu, 128), F32), pltpu.VMEM((12, 16 * na + 8, 128), F32),
            pltpu.VMEM((2, 8 * nu, 256), BF16), pltpu.VMEM((2, 8 * nu, 256), BF16),
            pltpu.VMEM((16, 8, 128), jnp.int32), pltpu.SMEM((16, 8, 128), jnp.int32),
            dma((3,)), dma((15,)), dma((16,)), dma((8,)), dma((8,)), dma((8,)), dma((8,)),
            dma((15,)), dma((16,)), dma((15,)), dma((16,)), dma((15,)), dma((16,)), dma,
        ],
        compiler_params=pltpu.CompilerParams(collective_id=0, has_side_effects=True, vmem_limit_bytes=56 << 20),
        name="galerkin",
    )(solution_modes.reshape(-1, 128), coefficient_modes.reshape(-1, 128), coupling[0], source_block, expansion_index)
    return out.reshape(solution_modes.shape)


def solution(mesh):
    placed = (
        P("modes", "tiles", None, None),
        P("modes", "tiles", None, None),
        P("modes", None, None, None),
        P("modes", None),
        P("modes", None),
    )
    return jax.shard_map(
        on_device,
        mesh=mesh,
        in_specs=placed,
        out_specs=P("modes", "tiles", None, None),
        check_vma=False,
    )
```

```python
import functools

import jax
import jax.numpy as jnp
from jax import lax
from jax.experimental import pallas as pl
from jax.experimental.pallas import tpu as pltpu
from jax.sharding import PartitionSpec as P

F32, BF16 = jnp.float32, jnp.bfloat16


def lanes(shape):
    return lax.broadcasted_iota(jnp.int32, shape, len(shape) - 1)


def difference(own, other):
    return own - other


def mean(own, other):
    return 0.5 * (own + other)


def kroll(value, shift):
    return pltpu.roll(value, shift, value.ndim - 1)


def transpose_blocks(rows):
    lane = lanes(rows[0].shape)
    for d in (1, 2, 4, 8):
        keep = (lane // 8) & d == 0
        fresh = list(rows)
        for i in range(16):
            if not i & d:
                fresh[i] = jnp.where(keep, rows[i], kroll(rows[i + d], 8 * d))
                fresh[i + d] = jnp.where(keep, kroll(rows[i], 128 - 8 * d), rows[i + d])
        rows = fresh
    return rows


def remote(src, dst, send, recv, **where):
    return pltpu.make_async_remote_copy(
        src_ref=src, dst_ref=dst, send_sem=send, recv_sem=recv,
        device_id=where, device_id_type=pl.DeviceIdType.MESH)


def greet(others):
    barrier = pltpu.get_barrier_semaphore()
    for where in others:
        pl.semaphore_signal(barrier, inc=1, device_id=where, device_id_type=pl.DeviceIdType.MESH)
    return barrier


def face_tiles(comb, x0, x1, below, above, r_minus, r_plus):
    lane = lanes(x0.shape)
    zz, yy, low = lane % 8, (lane // 8) % 8, lane < 64
    zero = jnp.zeros_like(x0)
    r0, r1 = kroll(x0, 64), kroll(x1, 64)
    yield comb(x0, jnp.where(low, r0, r1))
    yield comb(x1, jnp.where(low, r1, r_plus))
    yield comb(x0, jnp.where(low, r_minus, r0))
    yield comb(x1, jnp.where(low, r0, r1))
    for x in (x0, x1):
        yield comb(x, jnp.where(yy < 7, kroll(x, 120), zero))
    for x in (x0, x1):
        yield comb(x, jnp.where(yy > 0, kroll(x, 8), zero))
    for x, rim in zip((x0, x1), above):
        yield comb(x, jnp.where(zz < 7, kroll(x, 127), rim))
    for x, rim in zip((x0, x1), below):
        yield comb(x, jnp.where(zz > 0, kroll(x, 1), rim))


def cut(value_ref, pieces, count, first, span):
    def one(m, carry):
        for t in range(2):
            place = pl.ds(pl.multiple_of(span * t + first + 8 * m, 8), 8)
            rows = [value_ref[pl.ds(256 * m + 16 * t + i, 8, stride=32), :] for i in range(16)]
            for p, value in enumerate(transpose_blocks(rows)):
                pieces[p + 1, place] = value
        return carry

    lax.fori_loop(0, count // 8, one, 0)


def rims(pieces, nu, na):
    span = nu + na
    for q in (0, 17):
        pieces[q, pl.ds(0, 2 * span)] = jnp.zeros((2 * span, 128), F32)

    def one(p, carry):
        zz = lanes((8, 128)) % 8

        def rim(first, spots, base):
            for (t, side), spot in spots:
                value = pieces[p + 2 * side, pl.ds(span * t + first, 8)]
                shift = (spot - (0 if side else 7)) % 128
                base = jnp.where(zz == spot, kroll(value, shift), base)
            return base

        outer = (((0, 1), 7), ((1, 1), 6), ((0, 0), 0), ((1, 0), 1))
        inner = (((0, 1), 5), ((1, 1), 4), ((0, 0), 2), ((1, 0), 3))
        for m in range(nu // 16):
            value = rim(8 * m, outer, jnp.zeros((8, 128), F32))
            pieces[p + 1, pl.ds(2 * span + 8 * m, 8)] = rim(nu // 2 + 8 * m, inner, value)
        for m in range(na // 8):
            pieces[p + 1, pl.ds(2 * span + nu // 2 + 8 * m, 8)] = rim(nu + 8 * m, outer, jnp.zeros((8, 128), F32))
        return carry

    lax.fori_loop(0, 16, one, 0, unroll=2)


def pack(c_ref, held, me):
    n = c_ref.shape[1]
    for q in range(4):
        for h in range(2):
            for m in range(n // 8):
                parts = [c_ref[8 * q + 4 * h + l, pl.ds(8 * m, 8), :] for l in range(4)]
                held[me, pl.ds(n * q + 8 * m, 8), pl.ds(128 * h, 128)] = jnp.concatenate(parts, axis=1)


def kernel(u_hbm, a_hbm, c_hbm, sb_ref, ei_ref, out_ref,
           u_ref, a_ref, c_ref, pieces, got, up_out, down_out, from_down, from_up, held, part, back,
           delta, faces, mixed, index_v, index_s,
           in_sem, p_send, p_recv, m_send, m_recv, q_send, q_recv, c_send, c_recv, o_send, o_recv, i_send, i_recv, own_sem):
    me, tile = lax.axis_index("modes"), lax.axis_index("tiles")
    tiles = lax.axis_size("tiles")
    has_up, has_down = tile < tiles - 1, tile > 0
    z, y, core = me // 8, lax.rem(me // 2, 4), lax.rem(me, 2)
    nu, na = u_ref.shape[0] // 32, a_ref.shape[0] // 32
    span = nu + na
    slots = c_ref.shape[0]

    def block(dz, dy, dc):
        return lax.rem(z + dz, 2) * 8 + lax.rem(y + dy, 4) * 2 + lax.rem(core + dc, 2)

    loads = [pltpu.make_async_copy(s, d, in_sem.at[i])
             for i, (s, d) in enumerate(((u_hbm, u_ref), (a_hbm, a_ref), (c_hbm, c_ref)))]
    for load in loads:
        load.start()
    opposite = lax.rem(tile + tiles // 2, tiles)
    chips = ((0, 0), (0, 1), (0, 3), (1, 0), (0, 2), (1, 1), (1, 3), (1, 2))
    offsets = [(dz, dy, dc) for dz, dy in chips for dc in range(2)][1:]
    barrier = greet([{"modes": block(*o)} for o in offsets] + [{"modes": block(1, 0, 0), "tiles": opposite}])

    @pl.when(has_up)
    def _():
        pl.semaphore_signal(barrier, inc=1, device_id={"tiles": tile + 1}, device_id_type=pl.DeviceIdType.MESH)

    @pl.when(has_down)
    def _():
        pl.semaphore_signal(barrier, inc=1, device_id={"tiles": tile - 1}, device_id_type=pl.DeviceIdType.MESH)

    loads[0].wait()
    cut(u_ref, pieces, nu, 0, span)
    loads[1].wait()
    cut(a_ref, pieces, na, nu, span)
    rims(pieces, nu, na)
    index_v[me] = jnp.zeros((1, 128), jnp.int32)
    index_v[me, :, pl.ds(0, slots)] = sb_ref[...]
    index_v[me, :, pl.ds(slots, slots)] = ei_ref[...]

    @pl.when(jnp.logical_not(has_down))
    def _():
        from_down[...] = jnp.zeros(from_down.shape, F32)

    @pl.when(jnp.logical_not(has_up))
    def _():
        from_up[...] = jnp.zeros(from_up.shape, F32)

    pl.semaphore_wait(barrier, 16 + has_up.astype(jnp.int32) + has_down.astype(jnp.int32))

    own = pltpu.make_async_copy(pieces.at[me + 1], got.at[me], own_sem)
    own.start()
    sends = []
    for i, o in enumerate(offsets):
        copy = remote(pieces.at[block(*o) + 1], got.at[me], p_send.at[i], p_recv.at[me], modes=block(*o))
        copy.start()
        sends.append(copy)
    for i, o in enumerate(offsets):
        copy = remote(index_v.at[me], index_v.at[me], i_send.at[i], i_recv.at[me], modes=block(*o))
        copy.start()
        sends.append(copy)
    loads[2].wait()
    pack(c_ref, held, me)

    def upward(g):
        return remote(up_out.at[g], from_down.at[g], m_send.at[g], m_recv.at[g], tiles=tile + 1)

    def downward(g):
        return remote(down_out.at[g], from_up.at[g], q_send.at[g], q_recv.at[g], tiles=tile - 1)

    low = lanes((8, 128)) < 64
    own.wait()
    for dz, dy in chips:
        for dc in range(2):
            if (dz, dy, dc) != (0, 0, 0):
                source = block(dz, dy, dc)
                remote(pieces.at[1], got.at[source], p_send.at[0], p_recv.at[source], modes=source).wait_recv()
        g = block(dz, dy, 0) // 2
        for m in range(span // 8):
            first = pl.ds(8 * m, 8)
            second = pl.ds(span + 8 * m, 8)
            up_out[g, first] = jnp.where(low, kroll(got[2 * g, second], 64), got[2 * g + 1, second])
            down_out[g, first] = jnp.where(low, got[2 * g, first], kroll(got[2 * g + 1, first], 64))

        @pl.when(has_up)
        def _():
            upward(g).start()

        @pl.when(has_down)
        def _():
            downward(g).start()

    def share(i, which, modes, to):
        return remote(held.at[which], held.at[which], c_send.at[i], c_recv.at[which], modes=modes, tiles=to)

    share(0, me, block(0, 1, 0), tile).start()
    share(1, me, block(0, 3, 0), tile).start()
    share(2, me, block(1, 0, 0), tile).start()
    share(3, me, block(0, 0, 1), tile).start()
    for o in offsets:
        source = block(*o)
        remote(index_v.at[source], index_v.at[source], i_send.at[0], i_recv.at[source], modes=source).wait_recv()
    indices = pltpu.make_async_copy(index_v, index_s, own_sem)
    indices.start()

    def prepare(i, carry):
        dz, r = i // 4, i % 4
        g = block(dz, r + (r // 2) * (1 - 2 * (r % 2)), 0) // 2

        @pl.when(has_up)
        def _():
            remote(down_out.at[g], from_up.at[g], q_send.at[g], q_recv.at[g], tiles=tile + 1).wait_recv()

        @pl.when(has_down)
        def _():
            remote(up_out.at[g], from_down.at[g], m_send.at[g], m_recv.at[g], tiles=tile - 1).wait_recv()

        for odd in range(2):
            j = 2 * g + odd

            def tiles_of(first, rim, shifts):
                minus, plus = from_down[g, pl.ds(first, 8)], from_up[g, pl.ds(first, 8)]
                minus, plus = (kroll(minus, 64), plus) if odd else (minus, kroll(plus, 64))
                value = got[j, pl.ds(2 * span + rim, 8)]
                below = [kroll(value, s % 128) if s else value for s in shifts[:2]]
                above = [kroll(value, s % 128) if s else value for s in shifts[2:]]
                return got[j, pl.ds(first, 8)], got[j, pl.ds(span + first, 8)], below, above, minus, plus

            for m in range(nu // 8):
                lower = m < nu // 16
                rim = 8 * m if lower else 8 * m - nu // 2
                parts = tiles_of(8 * m, rim, (0, -1, 0, 1) if lower else (-2, -3, 2, 3))
                for f, value in enumerate(face_tiles(difference, *parts)):
                    delta[j, f, pl.ds(8 * m, 8)] = value
            place = pl.ds(pl.multiple_of(8 * j, 8), 8)
            for f, value in enumerate(face_tiles(mean, *tiles_of(nu, nu // 2, (0, -1, 0, 1)))):
                faces[f, place] = value
        return carry

    lax.fori_loop(0, 8, prepare, 0)
    indices.wait()

    def build(b, c, buffer):
        for s in range(8):
            slot = c * 8 + s
            j = index_s[b, 0, slot]
            k = index_s[b, 0, slots + slot]
            for t in range(2):
                coefficient = [faces[2 * f + t, pl.ds(k, 8, stride=0)] for f in range(6)]
                for m in range(nu // 16):
                    pair = []
                    for h in range(2):
                        rows = pl.ds(16 * m + 8 * h, 8)
                        w = coefficient[0] * delta[j, t, rows]
                        for f in range(1, 6):
                            w = w + coefficient[f] * delta[j, 2 * f + t, rows]
                        pair.append(w)
                    for h in range(2):
                        mixed[buffer, pl.ds(nu * s + 16 * m + 8 * h, 8), pl.ds(128 * t, 128)] = pair[h]

    def product(b, c, buffer):
        coupling = held[b, pl.ds(nu * c, nu)]
        high = coupling.astype(BF16)
        small = (coupling - high.astype(F32)).astype(BF16)
        w = mixed[buffer]
        w_high = w.astype(BF16)
        w_small = (w - w_high.astype(F32)).astype(BF16)
        both = jnp.dot(jnp.concatenate([high, small], axis=0), w_high, preferred_element_type=F32)
        return (both[:nu] + both[nu:]) + jnp.dot(high, w_small, preferred_element_type=F32)

    def number(i):
        k = i // 2
        r = (k % 4 + k // 4) % 4
        return k // 4, r + (r // 2) * (1 - 2 * (r % 2)), i % 2

    def landed(which):
        share(0, which, block(0, 0, 1), tile).wait_recv()

    def deliver(i):
        b = block(*number(i))
        return remote(part.at[b], back.at[me], o_send.at[i - 1], o_recv.at[me], modes=b)

    def advance(i, carry):
        dz, dy, dc = number(i)
        b = block(dz, dy, dc)

        partner = block(0, 0, 1)

        @pl.when(i == 2)
        def _():
            for n, dy in enumerate((1, 3)):
                landed(block(0, dy, 0))
                share(4 + n, block(0, dy, 0), partner, tile).start()
                share(6 + n, block(0, dy, 0), block(1, 0, 0), opposite).start()
            share(8, block(0, 3 - 2 * core, 0), block(0, 1 + 2 * core, 0), tile).start()

        @pl.when(jnp.logical_or(dc == 1, i > 5))
        def _():
            landed(b)

        @pl.when(jnp.logical_and(dc == 0, i > 7))
        def _():
            share(7 + i // 2, b, partner, tile).start()

        @pl.when(i == 6)
        def _():
            share(9, b, partner, tile).start()
            share(10, b, block(1, 0, 0), opposite).start()

        total = None
        for c in range(slots // 8):
            build(b, c, c % 2)
            term = product(b, c, c % 2)
            total = term if total is None else total + term
            if c == 0:
                @pl.when(i > 1)
                def _():
                    deliver(i - 1).start()

        part[b, 0] = total[:, :128]
        part[b, 1] = total[:, 128:]

        @pl.when(i == 0)
        def _():
            back[me, 0] = total[:, :128]
            back[me, 1] = total[:, 128:]

        return carry

    lax.fori_loop(0, 16, advance, 0)
    deliver(15).start()

    for dz, dy, dc in offsets:
        source = block(dz, dy, dc)
        remote(part.at[0], back.at[source], o_send.at[0], o_recv.at[source], modes=source).wait_recv()

    def restore(m, carry):
        place = pl.ds(pl.multiple_of(8 * m, 8), 8)
        for t in range(2):
            rows = [back[p, t, place] for p in range(16)]
            for i, value in enumerate(transpose_blocks(rows)):
                out_ref[pl.ds(256 * m + 16 * t + i, 8, stride=32), :] = value
        return carry

    lax.fori_loop(0, nu // 8, restore, 0)
    for copy in sends:
        copy.wait_send()
    for i in range(15):
        share(i, me, block(0, 0, 1), tile).wait_send()
        deliver(i + 1).wait_send()
    for g in range(8):
        @pl.when(has_up)
        def _():
            upward(g).wait_send()

        @pl.when(has_down)
        def _():
            downward(g).wait_send()


def on_device(solution_modes, coefficient_modes, coupling, source_block, expansion_index):
    nu, na = solution_modes.shape[0], coefficient_modes.shape[0]
    span, slots = nu + na, source_block.shape[1]
    rows = 2 * span + nu // 2 + na
    vmem = pl.BlockSpec(memory_space=pltpu.VMEM)
    hbm = pl.BlockSpec(memory_space=pltpu.HBM)
    dma = pltpu.SemaphoreType.DMA
    out = pl.pallas_call(
        kernel,
        out_shape=jax.ShapeDtypeStruct((nu * 32, 128), F32),
        in_specs=[hbm, hbm, hbm, vmem, vmem],
        out_specs=vmem,
        scratch_shapes=[
            pltpu.VMEM((nu * 32, 128), F32), pltpu.VMEM((na * 32, 128), F32), pltpu.VMEM((slots, nu, nu), F32),
            pltpu.VMEM((18, rows, 128), F32), pltpu.VMEM((16, rows, 128), F32),
            pltpu.VMEM((8, span, 128), F32), pltpu.VMEM((8, span, 128), F32),
            pltpu.VMEM((8, span, 128), F32), pltpu.VMEM((8, span, 128), F32),
            pltpu.VMEM((16, slots // 8 * nu, 256), F32),
            pltpu.VMEM((16, 2, nu, 128), F32), pltpu.VMEM((16, 2, nu, 128), F32),
            pltpu.VMEM((16, 12, nu, 128), F32), pltpu.VMEM((12, 16 * na + 8, 128), F32),
            pltpu.VMEM((2, 8 * nu, 256), F32),
            pltpu.VMEM((16, 1, 128), jnp.int32), pltpu.SMEM((16, 1, 128), jnp.int32),
            dma((3,)), dma((15,)), dma((16,)), dma((8,)), dma((8,)), dma((8,)), dma((8,)),
            dma((15,)), dma((16,)), dma((15,)), dma((16,)), dma((15,)), dma((16,)), dma,
        ],
        compiler_params=pltpu.CompilerParams(collective_id=0, has_side_effects=True, vmem_limit_bytes=24 << 20),
        name="galerkin",
    )(*(pltpu.with_memory_space_constraint(v, pltpu.HBM) for v in (
        solution_modes.reshape(-1, 128), coefficient_modes.reshape(-1, 128), coupling[0])), source_block, expansion_index)
    return out.reshape(solution_modes.shape)


def solution(mesh):
    placed = (
        P("modes", "tiles", None, None),
        P("modes", "tiles", None, None),
        P("modes", None, None, None),
        P("modes", None),
        P("modes", None),
    )
    return jax.shard_map(
        on_device,
        mesh=mesh,
        in_specs=placed,
        out_specs=P("modes", "tiles", None, None),
        check_vma=False,
    )
```

```python
import functools

import jax
import jax.numpy as jnp
from jax import lax
from jax.experimental import pallas as pl
from jax.experimental.pallas import tpu as pltpu
from jax.sharding import PartitionSpec as P

F32, BF16 = jnp.float32, jnp.bfloat16


def lanes(shape):
    return lax.broadcasted_iota(jnp.int32, shape, len(shape) - 1)


def difference(own, other):
    return own - other


def mean(own, other):
    return 0.5 * (own + other)


def kroll(value, shift):
    return pltpu.roll(value, shift, value.ndim - 1)


def transpose_blocks(rows):
    lane = lanes(rows[0].shape)
    for d in (1, 2, 4, 8):
        keep = (lane // 8) & d == 0
        fresh = list(rows)
        for i in range(16):
            if not i & d:
                fresh[i] = jnp.where(keep, rows[i], kroll(rows[i + d], 8 * d))
                fresh[i + d] = jnp.where(keep, kroll(rows[i], 128 - 8 * d), rows[i + d])
        rows = fresh
    return rows


def remote(src, dst, send, recv, **where):
    return pltpu.make_async_remote_copy(
        src_ref=src, dst_ref=dst, send_sem=send, recv_sem=recv,
        device_id=where, device_id_type=pl.DeviceIdType.MESH)


def greet(others):
    barrier = pltpu.get_barrier_semaphore()
    for where in others:
        pl.semaphore_signal(barrier, inc=1, device_id=where, device_id_type=pl.DeviceIdType.MESH)
    return barrier


def face_tiles(comb, x0, x1, below, above, r_minus, r_plus):
    lane = lanes(x0.shape)
    zz, yy, low = lane % 8, (lane // 8) % 8, lane < 64
    zero = jnp.zeros_like(x0)
    r0, r1 = kroll(x0, 64), kroll(x1, 64)
    yield comb(x0, jnp.where(low, r0, r1))
    yield comb(x1, jnp.where(low, r1, r_plus))
    yield comb(x0, jnp.where(low, r_minus, r0))
    yield comb(x1, jnp.where(low, r0, r1))
    for x in (x0, x1):
        yield comb(x, jnp.where(yy < 7, kroll(x, 120), zero))
    for x in (x0, x1):
        yield comb(x, jnp.where(yy > 0, kroll(x, 8), zero))
    for x, rim in zip((x0, x1), above):
        yield comb(x, jnp.where(zz < 7, kroll(x, 127), rim))
    for x, rim in zip((x0, x1), below):
        yield comb(x, jnp.where(zz > 0, kroll(x, 1), rim))


def cut(value_ref, pieces, count, first, span):
    def one(m, carry):
        for t in range(2):
            place = pl.ds(pl.multiple_of(span * t + first + 8 * m, 8), 8)
            rows = [value_ref[pl.ds(256 * m + 16 * t + i, 8, stride=32), :] for i in range(16)]
            for p, value in enumerate(transpose_blocks(rows)):
                pieces[p + 1, place] = value
        return carry

    lax.fori_loop(0, count // 8, one, 0)


def rims(pieces, nu, na):
    span = nu + na
    for q in (0, 17):
        pieces[q, pl.ds(0, 2 * span)] = jnp.zeros((2 * span, 128), F32)

    def one(p, carry):
        zz = lanes((8, 128)) % 8

        def rim(first, spots, base):
            for (t, side), spot in spots:
                value = pieces[p + 2 * side, pl.ds(span * t + first, 8)]
                shift = (spot - (0 if side else 7)) % 128
                base = jnp.where(zz == spot, kroll(value, shift), base)
            return base

        outer = (((0, 1), 7), ((1, 1), 6), ((0, 0), 0), ((1, 0), 1))
        inner = (((0, 1), 5), ((1, 1), 4), ((0, 0), 2), ((1, 0), 3))
        for m in range(nu // 16):
            value = rim(8 * m, outer, jnp.zeros((8, 128), F32))
            pieces[p + 1, pl.ds(2 * span + 8 * m, 8)] = rim(nu // 2 + 8 * m, inner, value)
        for m in range(na // 8):
            pieces[p + 1, pl.ds(2 * span + nu // 2 + 8 * m, 8)] = rim(nu + 8 * m, outer, jnp.zeros((8, 128), F32))
        return carry

    lax.fori_loop(0, 16, one, 0, unroll=2)


def pack(c_ref, held, me):
    n = c_ref.shape[1]
    for q in range(4):
        for h in range(2):
            for m in range(n // 8):
                parts = [c_ref[8 * q + 4 * h + l, pl.ds(8 * m, 8), :] for l in range(4)]
                held[me, pl.ds(n * q + 8 * m, 8), pl.ds(128 * h, 128)] = jnp.concatenate(parts, axis=1)


def kernel(u_hbm, a_hbm, c_hbm, sb_ref, ei_ref, out_ref,
           u_ref, a_ref, c_ref, pieces, got, up_out, down_out, from_down, from_up, held, part, back,
           delta, faces, mixed, index_v, index_s,
           in_sem, p_send, p_recv, m_send, m_recv, q_send, q_recv, c_send, c_recv, o_send, o_recv, i_send, i_recv, s_send, s_recv, own_sem):
    me, tile = lax.axis_index("modes"), lax.axis_index("tiles")
    tiles = lax.axis_size("tiles")
    has_up, has_down = tile < tiles - 1, tile > 0
    z, y, core = me // 8, lax.rem(me // 2, 4), lax.rem(me, 2)
    nu, na = u_ref.shape[0] // 32, a_ref.shape[0] // 32
    span = nu + na
    slots = c_ref.shape[0]

    def block(dz, dy, dc):
        return lax.rem(z + dz, 2) * 8 + lax.rem(y + dy, 4) * 2 + lax.rem(core + dc, 2)

    loads = [pltpu.make_async_copy(s, d, in_sem.at[i])
             for i, (s, d) in enumerate(((u_hbm, u_ref), (a_hbm, a_ref), (c_hbm, c_ref)))]
    for load in loads:
        load.start()
    row = tiles // 2
    opposite = lax.rem(tile + row, tiles)
    x = lax.rem(tile, row)
    beside = [tile - x + lax.rem(x + d, row) for d in range(1, row)]
    chips = ((0, 0), (0, 1), (0, 3), (1, 0), (0, 2), (1, 1), (1, 3), (1, 2))
    offsets = [(dz, dy, dc) for dz, dy in chips for dc in range(2)][1:]
    barrier = greet([{"modes": block(*o)} for o in offsets] + [{"modes": block(1, 0, 0), "tiles": opposite}]
                    + [{"tiles": t} for t in beside])
    wrap_up, wrap_down = has_up & (x == row - 1), has_down & (x == 0)

    @pl.when(wrap_up)
    def _():
        pl.semaphore_signal(barrier, inc=1, device_id={"tiles": tile + 1}, device_id_type=pl.DeviceIdType.MESH)

    @pl.when(wrap_down)
    def _():
        pl.semaphore_signal(barrier, inc=1, device_id={"tiles": tile - 1}, device_id_type=pl.DeviceIdType.MESH)

    loads[0].wait()
    cut(u_ref, pieces, nu, 0, span)
    loads[1].wait()
    cut(a_ref, pieces, na, nu, span)
    rims(pieces, nu, na)
    loads[2].wait()
    pack(c_ref, held, me)
    index_v[me] = jnp.zeros((1, 128), jnp.int32)
    index_v[me, :, pl.ds(0, slots)] = sb_ref[...]
    index_v[me, :, pl.ds(slots, slots)] = ei_ref[...]

    @pl.when(jnp.logical_not(has_down))
    def _():
        from_down[...] = jnp.zeros(from_down.shape, F32)

    @pl.when(jnp.logical_not(has_up))
    def _():
        from_up[...] = jnp.zeros(from_up.shape, F32)

    pl.semaphore_wait(barrier, 15 + row + wrap_up.astype(jnp.int32) + wrap_down.astype(jnp.int32))

    own = pltpu.make_async_copy(pieces.at[me + 1], got.at[me], own_sem)
    own.start()
    def share(i, which, modes, to):
        return remote(held.at[which], held.at[which], c_send.at[i], c_recv.at[which], modes=modes, tiles=to)

    def quarter(i, which, q, modes, to):
        place = held.at[which, pl.ds(pl.multiple_of(nu * q, nu), nu)]
        return remote(place, place, s_send.at[i], s_recv.at[which, q], modes=modes, tiles=to)

    partner = block(0, 0, 1)
    for i, dy in enumerate((1, 3, 2)):
        quarter(i, me, x, block(0, dy, 0), tile).start()
    share(0, me, block(1, 0, 0), opposite).start()
    share(1, me, partner, tile).start()
    sends = [remote(index_v.at[me], index_v.at[me], i_send.at[i], i_recv.at[me], modes=block(*o))
             for i, o in enumerate(offsets)]
    sends += [remote(pieces.at[block(*o) + 1], got.at[me], p_send.at[i], p_recv.at[me], modes=block(*o))
              for i, o in enumerate(offsets)]
    for copy in sends:
        copy.start()
    for n, dy in enumerate((1, 3, 2)):
        which = block(0, dy, 0)
        quarter(0, which, x, which, tile).wait_recv()
        for i, to in enumerate(beside):
            quarter(3 + 3 * n + i, which, x, me, to).start()
    for n, dy in enumerate((1, 3, 2)):
        which = block(0, dy, 0)
        for to in beside:
            quarter(0, which, lax.rem(to, row), me, to).wait_recv()
        share(2 + n, which, block(1, 0, 0), opposite).start()
        share(5 + n, which, partner, tile).start()

    def upward(g):
        return remote(up_out.at[g], from_down.at[g], m_send.at[g], m_recv.at[g], tiles=tile + 1)

    def downward(g):
        return remote(down_out.at[g], from_up.at[g], q_send.at[g], q_recv.at[g], tiles=tile - 1)

    low = lanes((8, 128)) < 64
    own.wait()
    for dz, dy in chips:
        for dc in range(2):
            if (dz, dy, dc) != (0, 0, 0):
                source = block(dz, dy, dc)
                remote(pieces.at[1], got.at[source], p_send.at[0], p_recv.at[source], modes=source).wait_recv()
        g = block(dz, dy, 0) // 2
        for m in range(span // 8):
            first = pl.ds(8 * m, 8)
            second = pl.ds(span + 8 * m, 8)
            up_out[g, first] = jnp.where(low, kroll(got[2 * g, second], 64), got[2 * g + 1, second])
            down_out[g, first] = jnp.where(low, got[2 * g, first], kroll(got[2 * g + 1, first], 64))

        @pl.when(has_up)
        def _():
            upward(g).start()

        @pl.when(has_down)
        def _():
            downward(g).start()

    for o in offsets:
        source = block(*o)
        remote(index_v.at[source], index_v.at[source], i_send.at[0], i_recv.at[source], modes=source).wait_recv()
    indices = pltpu.make_async_copy(index_v, index_s, own_sem)
    indices.start()

    def prepare(i, carry):
        dz, r = i // 4, i % 4
        g = block(dz, r + (r // 2) * (1 - 2 * (r % 2)), 0) // 2

        @pl.when(has_up)
        def _():
            remote(down_out.at[g], from_up.at[g], q_send.at[g], q_recv.at[g], tiles=tile + 1).wait_recv()

        @pl.when(has_down)
        def _():
            remote(up_out.at[g], from_down.at[g], m_send.at[g], m_recv.at[g], tiles=tile - 1).wait_recv()

        for odd in range(2):
            j = 2 * g + odd

            def tiles_of(first, rim, shifts):
                minus, plus = from_down[g, pl.ds(first, 8)], from_up[g, pl.ds(first, 8)]
                minus, plus = (kroll(minus, 64), plus) if odd else (minus, kroll(plus, 64))
                value = got[j, pl.ds(2 * span + rim, 8)]
                below = [kroll(value, s % 128) if s else value for s in shifts[:2]]
                above = [kroll(value, s % 128) if s else value for s in shifts[2:]]
                return got[j, pl.ds(first, 8)], got[j, pl.ds(span + first, 8)], below, above, minus, plus

            for m in range(nu // 8):
                lower = m < nu // 16
                rim = 8 * m if lower else 8 * m - nu // 2
                parts = tiles_of(8 * m, rim, (0, -1, 0, 1) if lower else (-2, -3, 2, 3))
                for f, value in enumerate(face_tiles(difference, *parts)):
                    delta[j, f, pl.ds(8 * m, 8)] = value
            place = pl.ds(pl.multiple_of(8 * j, 8), 8)
            for f, value in enumerate(face_tiles(mean, *tiles_of(nu, nu // 2, (0, -1, 0, 1)))):
                faces[f, place] = value
        return carry

    lax.fori_loop(0, 8, prepare, 0)
    indices.wait()

    def build(b, c, buffer):
        for s in range(8):
            slot = c * 8 + s
            j = index_s[b, 0, slot]
            k = index_s[b, 0, slots + slot]
            for t in range(2):
                coefficient = [faces[2 * f + t, pl.ds(k, 8, stride=0)] for f in range(6)]
                for m in range(nu // 16):
                    pair = []
                    for h in range(2):
                        rows = pl.ds(16 * m + 8 * h, 8)
                        w = coefficient[0] * delta[j, t, rows]
                        for f in range(1, 6):
                            w = w + coefficient[f] * delta[j, 2 * f + t, rows]
                        pair.append(w)
                    for h in range(2):
                        mixed[buffer, pl.ds(nu * s + 16 * m + 8 * h, 8), pl.ds(128 * t, 128)] = pair[h]

    def product(b, c, buffer):
        coupling = held[b, pl.ds(nu * c, nu)]
        high = coupling.astype(BF16)
        small = (coupling - high.astype(F32)).astype(BF16)
        w = mixed[buffer]
        w_high = w.astype(BF16)
        w_small = (w - w_high.astype(F32)).astype(BF16)
        both = jnp.dot(jnp.concatenate([high, small], axis=0), w_high, preferred_element_type=F32)
        return (both[:nu] + both[nu:]) + jnp.dot(high, w_small, preferred_element_type=F32)

    def number(k):
        k = (k + 1) % 8
        r = k % 4
        return k // 4, r + (r // 2) * (1 - 2 * (r % 2))

    def landed(which):
        share(0, which, partner, tile).wait_recv()

    def deliver(i, b):
        return remote(part.at[b], back.at[me], o_send.at[i], o_recv.at[me], modes=b)

    def advance(k, carry):
        dz, dy = number(k)
        ahead = block(*number(k + 1), 0)
        own_block, other_block = block(dz, dy, 0), block(dz, dy, 1)

        @pl.when(k > 0)
        def _():
            last = number(k + 7)
            deliver(2 * k - 2, block(*last, 0)).start()
            deliver(2 * k - 1, block(*last, 1)).start()

        @pl.when((k > 1) & (k < 6))
        def _():
            landed(ahead)
            share(6 + k, ahead, partner, tile).start()

        landed(other_block)
        totals = []
        for h, b in enumerate((own_block, other_block)):
            total = None
            for c in range(slots // 8):
                build(b, c, c % 2)
                term = product(b, c, c % 2)
                total = term if total is None else total + term
            totals.append(total)
            for t in range(2):
                part[b, t] = total[:, 128 * t:128 * (t + 1)]

        @pl.when(k == 7)
        def _():
            for t in range(2):
                back[me, t] = totals[0][:, 128 * t:128 * (t + 1)]

        return carry

    lax.fori_loop(0, 8, advance, 0)
    deliver(14, partner).start()

    for dz, dy, dc in offsets:
        source = block(dz, dy, dc)
        remote(part.at[0], back.at[source], o_send.at[0], o_recv.at[source], modes=source).wait_recv()

    def restore(m, carry):
        place = pl.ds(pl.multiple_of(8 * m, 8), 8)
        for t in range(2):
            rows = [back[p, t, place] for p in range(16)]
            for i, value in enumerate(transpose_blocks(rows)):
                out_ref[pl.ds(256 * m + 16 * t + i, 8, stride=32), :] = value
        return carry

    lax.fori_loop(0, nu // 8, restore, 0)
    for copy in sends:
        copy.wait_send()
    for i in range(12):
        share(i, me, partner, tile).wait_send()
        quarter(i, me, x, partner, tile).wait_send()
    for i in range(15):
        deliver(i, partner).wait_send()
    for g in range(8):
        @pl.when(has_up)
        def _():
            upward(g).wait_send()

        @pl.when(has_down)
        def _():
            downward(g).wait_send()


def on_device(solution_modes, coefficient_modes, coupling, source_block, expansion_index):
    nu, na = solution_modes.shape[0], coefficient_modes.shape[0]
    span, slots = nu + na, source_block.shape[1]
    rows = 2 * span + nu // 2 + na
    vmem = pl.BlockSpec(memory_space=pltpu.VMEM)
    hbm = pl.BlockSpec(memory_space=pltpu.HBM)
    dma = pltpu.SemaphoreType.DMA
    out = pl.pallas_call(
        kernel,
        out_shape=jax.ShapeDtypeStruct((nu * 32, 128), F32),
        in_specs=[hbm, hbm, hbm, vmem, vmem],
        out_specs=vmem,
        scratch_shapes=[
            pltpu.VMEM((nu * 32, 128), F32), pltpu.VMEM((na * 32, 128), F32), pltpu.VMEM((slots, nu, nu), F32),
            pltpu.VMEM((18, rows, 128), F32), pltpu.VMEM((16, rows, 128), F32),
            pltpu.VMEM((8, span, 128), F32), pltpu.VMEM((8, span, 128), F32),
            pltpu.VMEM((8, span, 128), F32), pltpu.VMEM((8, span, 128), F32),
            pltpu.VMEM((16, slots // 8 * nu, 256), F32),
            pltpu.VMEM((16, 2, nu, 128), F32), pltpu.VMEM((16, 2, nu, 128), F32),
            pltpu.VMEM((16, 12, nu, 128), F32), pltpu.VMEM((12, 16 * na + 8, 128), F32),
            pltpu.VMEM((2, 8 * nu, 256), F32),
            pltpu.VMEM((16, 1, 128), jnp.int32), pltpu.SMEM((16, 1, 128), jnp.int32),
            dma((3,)), dma((15,)), dma((16,)), dma((8,)), dma((8,)), dma((8,)), dma((8,)),
            dma((12,)), dma((16,)), dma((15,)), dma((16,)), dma((15,)), dma((16,)), dma((12,)), dma((16, 4)), dma,
        ],
        compiler_params=pltpu.CompilerParams(collective_id=0, has_side_effects=True, vmem_limit_bytes=24 << 20),
        name="galerkin",
    )(*(pltpu.with_memory_space_constraint(v, pltpu.HBM) for v in (
        solution_modes.reshape(-1, 128), coefficient_modes.reshape(-1, 128), coupling[0])), source_block, expansion_index)
    return out.reshape(solution_modes.shape)


def solution(mesh):
    placed = (
        P("modes", "tiles", None, None),
        P("modes", "tiles", None, None),
        P("modes", None, None, None),
        P("modes", None),
        P("modes", None),
    )
    return jax.shard_map(
        on_device,
        mesh=mesh,
        in_specs=placed,
        out_specs=P("modes", "tiles", None, None),
        check_vma=False,
    )
```

```python
import functools

import jax
import jax.numpy as jnp
from jax import lax
from jax.experimental import pallas as pl
from jax.experimental.pallas import tpu as pltpu
from jax.sharding import PartitionSpec as P

F32, BF16 = jnp.float32, jnp.bfloat16


def lanes(shape):
    return lax.broadcasted_iota(jnp.int32, shape, len(shape) - 1)


def difference(own, other):
    return own - other


def mean(own, other):
    return 0.5 * (own + other)


def kroll(value, shift):
    return pltpu.roll(value, shift, value.ndim - 1)


def transpose_blocks(rows):
    lane = lanes(rows[0].shape)
    for d in (1, 2, 4, 8):
        keep = (lane // 8) & d == 0
        fresh = list(rows)
        for i in range(16):
            if not i & d:
                fresh[i] = jnp.where(keep, rows[i], kroll(rows[i + d], 8 * d))
                fresh[i + d] = jnp.where(keep, kroll(rows[i], 128 - 8 * d), rows[i + d])
        rows = fresh
    return rows


def remote(src, dst, send, recv, **where):
    return pltpu.make_async_remote_copy(
        src_ref=src, dst_ref=dst, send_sem=send, recv_sem=recv,
        device_id=where, device_id_type=pl.DeviceIdType.MESH)


def greet(others):
    barrier = pltpu.get_barrier_semaphore()
    for where in others:
        pl.semaphore_signal(barrier, inc=1, device_id=where, device_id_type=pl.DeviceIdType.MESH)
    return barrier


def face_tiles(comb, x0, x1, below, above, r_minus, r_plus):
    lane = lanes(x0.shape)
    zz, yy, low = lane % 8, (lane // 8) % 8, lane < 64
    zero = jnp.zeros_like(x0)
    r0, r1 = kroll(x0, 64), kroll(x1, 64)
    yield comb(x0, jnp.where(low, r0, r1))
    yield comb(x1, jnp.where(low, r1, r_plus))
    yield comb(x0, jnp.where(low, r_minus, r0))
    yield comb(x1, jnp.where(low, r0, r1))
    for x in (x0, x1):
        yield comb(x, jnp.where(yy < 7, kroll(x, 120), zero))
    for x in (x0, x1):
        yield comb(x, jnp.where(yy > 0, kroll(x, 8), zero))
    for x, rim in zip((x0, x1), above):
        yield comb(x, jnp.where(zz < 7, kroll(x, 127), rim))
    for x, rim in zip((x0, x1), below):
        yield comb(x, jnp.where(zz > 0, kroll(x, 1), rim))


def cut(value_ref, pieces, count, first, span):
    def one(m, carry):
        for t in range(2):
            place = pl.ds(pl.multiple_of(span * t + first + 8 * m, 8), 8)
            rows = [value_ref[pl.ds(256 * m + 16 * t + i, 8, stride=32), :] for i in range(16)]
            for p, value in enumerate(transpose_blocks(rows)):
                pieces[p, place] = value
        return carry

    lax.fori_loop(0, count // 8, one, 0, unroll=2 if count > 8 else 1)


def pack(c_ref, held, me):
    n = c_ref.shape[1]
    for q in range(4):
        for h in range(2):
            for m in range(n // 8):
                parts = [c_ref[8 * q + 4 * h + l, pl.ds(8 * m, 8), :] for l in range(4)]
                held[me, pl.ds(n * q + 8 * m, 8), pl.ds(128 * h, 128)] = jnp.concatenate(parts, axis=1)


def kernel(u_hbm, a_hbm, c_hbm, sb_hbm, ei_hbm, out_ref,
           u_ref, a_ref, c_ref, sb_ref, ei_ref, pieces, got, up_out, down_out, from_down, from_up,
           next_out, last_out, from_last, from_next, held, part, back,
           delta, faces, mixed, index_v, index_s,
           in_sem, p_send, p_recv, m_send, m_recv, q_send, q_recv,
           n_send, n_recv, l_send, l_recv, c_send, c_recv, o_send, o_recv, i_send, i_recv, s_send, s_recv, own_sem):
    me, tile = lax.axis_index("modes"), lax.axis_index("tiles")
    tiles = lax.axis_size("tiles")
    has_up, has_down = tile < tiles - 1, tile > 0
    has_next, has_last = me < 15, me > 0
    z, y, core = me // 8, lax.rem(me // 2, 4), lax.rem(me, 2)
    nu, na = u_ref.shape[0] // 32, a_ref.shape[0] // 32
    span = nu + na
    slots = c_ref.shape[0]

    def block(dz, dy, dc):
        return lax.rem(z + dz, 2) * 8 + lax.rem(y + dy, 4) * 2 + lax.rem(core + dc, 2)

    loads = [pltpu.make_async_copy(s, d, in_sem.at[i])
             for i, (s, d) in enumerate(((u_hbm, u_ref), (a_hbm, a_ref), (c_hbm, c_ref), (sb_hbm, sb_ref), (ei_hbm, ei_ref)))]
    for load in loads:
        load.start()
    row = tiles // 2
    opposite = lax.rem(tile + row, tiles)
    x = lax.rem(tile, row)
    beside = [tile - x + lax.rem(x + d, row) for d in range(1, row)]
    chips = ((0, 0), (0, 1), (0, 3), (1, 0), (0, 2), (1, 1), (1, 3), (1, 2))
    offsets = [(dz, dy, dc) for dz, dy in chips for dc in range(2)][1:]
    barrier = greet([{"modes": block(*o)} for o in offsets] + [{"modes": block(1, 0, 0), "tiles": opposite}]
                    + [{"tiles": t} for t in beside])
    wrap_up, wrap_down = has_up & (x == row - 1), has_down & (x == 0)

    @pl.when(wrap_up)
    def _():
        pl.semaphore_signal(barrier, inc=1, device_id={"tiles": tile + 1}, device_id_type=pl.DeviceIdType.MESH)

    @pl.when(wrap_down)
    def _():
        pl.semaphore_signal(barrier, inc=1, device_id={"tiles": tile - 1}, device_id_type=pl.DeviceIdType.MESH)

    loads[0].wait()
    cut(u_ref, pieces, nu, 0, span)
    loads[1].wait()
    cut(a_ref, pieces, na, nu, span)
    for load in loads[2:]:
        load.wait()
    pack(c_ref, held, me)
    index_v[me] = jnp.zeros((1, 128), jnp.int32)
    index_v[me, :, pl.ds(0, slots)] = sb_ref[...]
    index_v[me, :, pl.ds(slots, slots)] = ei_ref[...]

    @pl.when(jnp.logical_not(has_down))
    def _():
        from_down[...] = jnp.zeros(from_down.shape, F32)

    @pl.when(jnp.logical_not(has_up))
    def _():
        from_up[...] = jnp.zeros(from_up.shape, F32)

    @pl.when(jnp.logical_not(has_last))
    def _():
        from_last[...] = jnp.zeros(from_last.shape, F32)

    @pl.when(jnp.logical_not(has_next))
    def _():
        from_next[...] = jnp.zeros(from_next.shape, F32)

    pl.semaphore_wait(barrier, 15 + row + wrap_up.astype(jnp.int32) + wrap_down.astype(jnp.int32))

    own = pltpu.make_async_copy(pieces.at[me], got.at[me], own_sem)
    own.start()
    def share(i, which, modes, to):
        return remote(held.at[which], held.at[which], c_send.at[i], c_recv.at[which], modes=modes, tiles=to)

    def quarter(i, which, q, modes, to):
        place = held.at[which, pl.ds(pl.multiple_of(nu * q, nu), nu)]
        return remote(place, place, s_send.at[i], s_recv.at[which, q], modes=modes, tiles=to)

    partner = block(0, 0, 1)
    for i, dy in enumerate((1, 3, 2)):
        quarter(i, me, x, block(0, dy, 0), tile).start()
    share(0, me, block(1, 0, 0), opposite).start()
    share(1, me, partner, tile).start()
    sends = [remote(index_v.at[me], index_v.at[me], i_send.at[i], i_recv.at[me], modes=block(*o))
             for i, o in enumerate(offsets)]
    sends += [remote(pieces.at[block(*o)], got.at[me], p_send.at[i], p_recv.at[me], modes=block(*o))
              for i, o in enumerate(offsets)]
    for copy in sends:
        copy.start()
    for n, dy in enumerate((1, 3, 2)):
        which = block(0, dy, 0)
        quarter(0, which, x, which, tile).wait_recv()
        for i, to in enumerate(beside):
            quarter(3 + 3 * n + i, which, x, me, to).start()
    def upward(g):
        return remote(up_out.at[g], from_down.at[g], m_send.at[g], m_recv.at[g], tiles=tile + 1)

    def downward(g):
        return remote(down_out.at[g], from_up.at[g], q_send.at[g], q_recv.at[g], tiles=tile - 1)

    def onward(g):
        return remote(next_out.at[g], from_last.at[g], n_send.at[g], n_recv.at[g], modes=me + 1)

    def backward(g):
        return remote(last_out.at[g], from_next.at[g], l_send.at[g], l_recv.at[g], modes=me - 1)

    lane = lanes((8, 128))
    low, zz = lane < 64, lane % 8
    own.wait()
    for dz, dy in chips:
        for dc in range(2):
            if (dz, dy, dc) != (0, 0, 0):
                source = block(dz, dy, dc)
                remote(pieces.at[1], got.at[source], p_send.at[0], p_recv.at[source], modes=source).wait_recv()
        g = block(dz, dy, 0) // 2
        for m in range(span // 8):
            first = pl.ds(8 * m, 8)
            second = pl.ds(span + 8 * m, 8)
            e0, e1, o0, o1 = got[2 * g, first], got[2 * g, second], got[2 * g + 1, first], got[2 * g + 1, second]
            up_out[g, first] = jnp.where(low, kroll(e1, 64), o1)
            down_out[g, first] = jnp.where(low, e0, kroll(o0, 64))
            rim = jnp.where(zz == 2, kroll(o0, 123), kroll(o1, 124))
            next_out[g, first] = jnp.where(zz == 0, kroll(e0, 121), jnp.where(zz == 1, kroll(e1, 122), rim))
            rim = jnp.where(zz == 5, kroll(o0, 5), kroll(o1, 4))
            last_out[g, first] = jnp.where(zz == 7, kroll(e0, 7), jnp.where(zz == 6, kroll(e1, 6), rim))

        @pl.when(has_up)
        def _():
            upward(g).start()

        @pl.when(has_down)
        def _():
            downward(g).start()

        @pl.when(has_next)
        def _():
            onward(g).start()

        @pl.when(has_last)
        def _():
            backward(g).start()

    for n, dy in enumerate((1, 3, 2)):
        which = block(0, dy, 0)
        for to in beside:
            quarter(0, which, lax.rem(to, row), me, to).wait_recv()
        share(2 + n, which, block(1, 0, 0), opposite).start()
        share(5 + n, which, partner, tile).start()

    for o in offsets:
        source = block(*o)
        remote(index_v.at[source], index_v.at[source], i_send.at[0], i_recv.at[source], modes=source).wait_recv()
    indices = pltpu.make_async_copy(index_v, index_s, own_sem)
    indices.start()

    def prepare(i, carry):
        dz, r = i // 4, i % 4
        g = block(dz, r + (r // 2) * (1 - 2 * (r % 2)), 0) // 2

        @pl.when(has_up)
        def _():
            remote(down_out.at[g], from_up.at[g], q_send.at[g], q_recv.at[g], tiles=tile + 1).wait_recv()

        @pl.when(has_down)
        def _():
            remote(up_out.at[g], from_down.at[g], m_send.at[g], m_recv.at[g], tiles=tile - 1).wait_recv()

        @pl.when(has_last)
        def _():
            remote(next_out.at[g], from_last.at[g], n_send.at[g], n_recv.at[g], modes=me - 1).wait_recv()

        @pl.when(has_next)
        def _():
            remote(last_out.at[g], from_next.at[g], l_send.at[g], l_recv.at[g], modes=me + 1).wait_recv()

        for odd in range(2):
            j = 2 * g + odd

            def tiles_of(first):
                place = pl.ds(first, 8)
                minus, plus = from_down[g, place], from_up[g, place]
                minus, plus = (kroll(minus, 64), plus) if odd else (minus, kroll(plus, 64))
                below, above = from_last[g, place], from_next[g, place]
                below = [kroll(below, 128 - n) if n else below for n in (2 * odd, 2 * odd + 1)]
                above = [kroll(above, n) if n else above for n in (2 * odd, 2 * odd + 1)]
                return got[j, place], got[j, pl.ds(span + first, 8)], below, above, minus, plus

            for m in range(nu // 8):
                for f, value in enumerate(face_tiles(difference, *tiles_of(8 * m))):
                    delta[j, f, pl.ds(8 * m, 8)] = value
            place = pl.ds(pl.multiple_of(8 * j, 8), 8)
            for f, value in enumerate(face_tiles(mean, *tiles_of(nu))):
                faces[f, place] = value
        return carry

    lax.fori_loop(0, 8, prepare, 0)
    indices.wait()

    def build(b, c, buffer):
        for s in range(8):
            slot = c * 8 + s
            j = index_s[b, 0, slot]
            k = index_s[b, 0, slots + slot]
            for t in range(2):
                coefficient = [faces[2 * f + t, pl.ds(k, 8, stride=0)] for f in range(6)]
                for m in range(nu // 16):
                    pair = []
                    for h in range(2):
                        rows = pl.ds(16 * m + 8 * h, 8)
                        w = coefficient[0] * delta[j, t, rows]
                        for f in range(1, 6):
                            w = w + coefficient[f] * delta[j, 2 * f + t, rows]
                        pair.append(w)
                    for h in range(2):
                        mixed[buffer, pl.ds(nu * s + 16 * m + 8 * h, 8), pl.ds(128 * t, 128)] = pair[h]

    def product(b, c, buffer):
        coupling = held[b, pl.ds(nu * c, nu)]
        high = coupling.astype(BF16)
        small = (coupling - high.astype(F32)).astype(BF16)
        w = mixed[buffer]
        w_high = w.astype(BF16)
        w_small = (w - w_high.astype(F32)).astype(BF16)
        both = jnp.dot(jnp.concatenate([high, small], axis=0), w_high, preferred_element_type=F32)
        return (both[:nu] + both[nu:]) + jnp.dot(high, w_small, preferred_element_type=F32)

    def number(k):
        k = (k + 1) % 8
        r = k % 4
        return k // 4, r + (r // 2) * (1 - 2 * (r % 2))

    def landed(which):
        share(0, which, partner, tile).wait_recv()

    def deliver(i, b):
        return remote(part.at[b], back.at[me], o_send.at[i], o_recv.at[me], modes=b)

    def advance(k, carry):
        dz, dy = number(k)
        ahead = block(*number(k + 1), 0)
        own_block, other_block = block(dz, dy, 0), block(dz, dy, 1)

        @pl.when(k > 0)
        def _():
            last = number(k + 7)
            deliver(2 * k - 2, block(*last, 0)).start()
            deliver(2 * k - 1, block(*last, 1)).start()

        @pl.when((k > 1) & (k < 6))
        def _():
            landed(ahead)
            share(6 + k, ahead, partner, tile).start()

        landed(other_block)
        totals = []
        for h, b in enumerate((own_block, other_block)):
            total = None
            for c in range(slots // 8):
                build(b, c, c % 2)
                term = product(b, c, c % 2)
                total = term if total is None else total + term
            totals.append(total)
            for t in range(2):
                part[b, t] = total[:, 128 * t:128 * (t + 1)]

        @pl.when(k == 7)
        def _():
            for t in range(2):
                back[me, t] = totals[0][:, 128 * t:128 * (t + 1)]

        return carry

    lax.fori_loop(0, 8, advance, 0)
    deliver(14, partner).start()

    for dz, dy, dc in offsets:
        source = block(dz, dy, dc)
        remote(part.at[0], back.at[source], o_send.at[0], o_recv.at[source], modes=source).wait_recv()

    def restore(m, carry):
        place = pl.ds(pl.multiple_of(8 * m, 8), 8)
        for t in range(2):
            rows = [back[p, t, place] for p in range(16)]
            for i, value in enumerate(transpose_blocks(rows)):
                out_ref[pl.ds(256 * m + 16 * t + i, 8, stride=32), :] = value
        return carry

    lax.fori_loop(0, nu // 8, restore, 0, unroll=2)
    for copy in sends:
        copy.wait_send()
    for i in range(12):
        share(i, me, partner, tile).wait_send()
        quarter(i, me, x, partner, tile).wait_send()
    for i in range(15):
        deliver(i, partner).wait_send()
    for g in range(8):
        @pl.when(has_up)
        def _():
            upward(g).wait_send()

        @pl.when(has_down)
        def _():
            downward(g).wait_send()

        @pl.when(has_next)
        def _():
            onward(g).wait_send()

        @pl.when(has_last)
        def _():
            backward(g).wait_send()


def on_device(solution_modes, coefficient_modes, coupling, source_block, expansion_index):
    nu, na = solution_modes.shape[0], coefficient_modes.shape[0]
    span, slots = nu + na, source_block.shape[1]
    rows = 2 * span
    vmem = pl.BlockSpec(memory_space=pltpu.VMEM)
    hbm = pl.BlockSpec(memory_space=pltpu.HBM)
    dma = pltpu.SemaphoreType.DMA
    out = pl.pallas_call(
        kernel,
        out_shape=jax.ShapeDtypeStruct((nu * 32, 128), F32),
        in_specs=[hbm] * 5,
        out_specs=vmem,
        scratch_shapes=[
            pltpu.VMEM((nu * 32, 128), F32), pltpu.VMEM((na * 32, 128), F32), pltpu.VMEM((slots, nu, nu), F32),
            pltpu.VMEM((1, slots), jnp.int32), pltpu.VMEM((1, slots), jnp.int32),
            pltpu.VMEM((16, rows, 128), F32), pltpu.VMEM((16, rows, 128), F32),
            *[pltpu.VMEM((8, span, 128), F32)] * 8,
            pltpu.VMEM((16, slots // 8 * nu, 256), F32),
            pltpu.VMEM((16, 2, nu, 128), F32), pltpu.VMEM((16, 2, nu, 128), F32),
            pltpu.VMEM((16, 12, nu, 128), F32), pltpu.VMEM((12, 16 * na + 8, 128), F32),
            pltpu.VMEM((2, 8 * nu, 256), F32),
            pltpu.VMEM((16, 1, 128), jnp.int32), pltpu.SMEM((16, 1, 128), jnp.int32),
            dma((5,)), dma((15,)), dma((16,)), *[dma((8,))] * 8,
            dma((12,)), dma((16,)), dma((15,)), dma((16,)), dma((15,)), dma((16,)), dma((12,)), dma((16, 4)), dma,
        ],
        compiler_params=pltpu.CompilerParams(collective_id=0, has_side_effects=True, vmem_limit_bytes=24 << 20),
        name="galerkin",
    )(*(pltpu.with_memory_space_constraint(v, pltpu.HBM) for v in (
        solution_modes.reshape(-1, 128), coefficient_modes.reshape(-1, 128), coupling[0],
        source_block, expansion_index)))
    return out.reshape(solution_modes.shape)


def solution(mesh):
    placed = (
        P("modes", "tiles", None, None),
        P("modes", "tiles", None, None),
        P("modes", None, None, None),
        P("modes", None),
        P("modes", None),
    )
    return jax.shard_map(
        on_device,
        mesh=mesh,
        in_specs=placed,
        out_specs=P("modes", "tiles", None, None),
        check_vma=False,
    )
```

```python
import functools

import jax
import jax.numpy as jnp
from jax import lax
from jax.experimental import pallas as pl
from jax.experimental.pallas import tpu as pltpu
from jax.sharding import PartitionSpec as P

F32, BF16 = jnp.float32, jnp.bfloat16


def lanes(shape):
    return lax.broadcasted_iota(jnp.int32, shape, len(shape) - 1)


def difference(own, other):
    return own - other


def mean(own, other):
    return 0.5 * (own + other)


def kroll(value, shift):
    return pltpu.roll(value, shift, value.ndim - 1)


def transpose_blocks(rows, steps=(1, 2, 4, 8)):
    lane = lanes(rows[0].shape)
    for d in steps:
        keep = (lane // 8) & d == 0
        fresh = list(rows)
        for i in range(len(rows)):
            if not i & d:
                fresh[i] = jnp.where(keep, rows[i], kroll(rows[i + d], 8 * d))
                fresh[i + d] = jnp.where(keep, kroll(rows[i], 128 - 8 * d), rows[i + d])
        rows = fresh
    return rows


def remote(src, dst, send, recv, **where):
    return pltpu.make_async_remote_copy(
        src_ref=src, dst_ref=dst, send_sem=send, recv_sem=recv,
        device_id=where, device_id_type=pl.DeviceIdType.MESH)


def greet(others):
    barrier = pltpu.get_barrier_semaphore()
    for where in others:
        pl.semaphore_signal(barrier, inc=1, device_id=where, device_id_type=pl.DeviceIdType.MESH)
    return barrier


def inner_faces(comb, x0, x1):
    lane = lanes(x0.shape)
    yy, low = (lane // 8) % 8, lane < 64
    zero = jnp.zeros_like(x0)
    r0, r1 = kroll(x0, 64), kroll(x1, 64)
    swapped = jnp.where(low, r0, r1)
    yield 0, comb(x0, swapped)
    yield 3, comb(x1, swapped)
    for t, value in enumerate((x0, x1)):
        yield 4 + t, comb(value, jnp.where(yy < 7, kroll(value, 120), zero))
        yield 6 + t, comb(value, jnp.where(yy > 0, kroll(value, 8), zero))


def outer_faces(comb, x0, x1, below, above, r_minus, r_plus):
    lane = lanes(x0.shape)
    zz, low = lane % 8, lane < 64
    yield 1, comb(x1, jnp.where(low, kroll(x1, 64), r_plus))
    yield 2, comb(x0, jnp.where(low, r_minus, kroll(x0, 64)))
    for t, value in enumerate((x0, x1)):
        yield 8 + t, comb(value, jnp.where(zz < 7, kroll(value, 127), above[t]))
        yield 10 + t, comb(value, jnp.where(zz > 0, kroll(value, 1), below[t]))


def cut(value_ref, pieces, count, first, span):
    def one(m, carry):
        for t in range(2):
            place = pl.ds(pl.multiple_of(span * t + first + 8 * m, 8), 8)
            rows = [value_ref[pl.ds(256 * m + 16 * t + i, 8, stride=32), :] for i in range(16)]
            for p, value in enumerate(transpose_blocks(rows)):
                pieces[p, place] = value
        return carry

    lax.fori_loop(0, count // 8, one, 0, unroll=1)


def pack(c_ref, held, me):
    n = c_ref.shape[1]
    for q in range(4):
        for h in range(2):
            for m in range(n // 8):
                parts = [c_ref[8 * q + 4 * h + l, pl.ds(8 * m, 8), :] for l in range(4)]
                held[me, pl.ds(n * q + 8 * m, 8), pl.ds(128 * h, 128)] = jnp.concatenate(parts, axis=1)


def kernel(u_hbm, a_hbm, c_hbm, sb_hbm, ei_hbm, out_ref,
           u_ref, a_ref, c_ref, sb_ref, ei_ref, pieces, got, up_out, down_out, from_down, from_up,
           next_out, last_out, from_last, from_next, held, part, back,
           delta, faces, mixed, index_v, index_s,
           in_sem, p_send, p_recv, m_send, m_recv, q_send, q_recv,
           n_send, n_recv, l_send, l_recv, c_send, c_recv, o_send, o_recv, i_send, i_recv, s_send, s_recv, own_sem):
    me, tile = lax.axis_index("modes"), lax.axis_index("tiles")
    tiles = lax.axis_size("tiles")
    has_up, has_down = tile < tiles - 1, tile > 0
    has_next, has_last = me < 15, me > 0
    z, y, core = me // 8, lax.rem(me // 2, 4), lax.rem(me, 2)
    nu, na = u_ref.shape[0] // 32, a_ref.shape[0] // 32
    span = nu + na
    slots = c_ref.shape[0]

    def block(dz, dy, dc):
        return lax.rem(z + dz, 2) * 8 + lax.rem(y + dy, 4) * 2 + lax.rem(core + dc, 2)

    loads = [pltpu.make_async_copy(s, d, in_sem.at[i])
             for i, (s, d) in enumerate(((u_hbm, u_ref), (a_hbm, a_ref), (c_hbm, c_ref), (sb_hbm, sb_ref), (ei_hbm, ei_ref)))]
    for load in loads:
        load.start()
    row = tiles // 2
    opposite = lax.rem(tile + row, tiles)
    x = lax.rem(tile, row)
    beside = [tile - x + lax.rem(x + d, row) for d in range(1, row)]
    chips = ((0, 0), (0, 1), (0, 3), (1, 0), (0, 2), (1, 1), (1, 3), (1, 2))
    offsets = [(dz, dy, dc) for dz, dy in chips for dc in range(2)][1:]
    barrier = greet([{"modes": block(*o)} for o in offsets] + [{"modes": block(1, 0, 0), "tiles": opposite}]
                    + [{"tiles": t} for t in beside])
    wrap_up, wrap_down = has_up & (x == row - 1), has_down & (x == 0)

    @pl.when(wrap_up)
    def _():
        pl.semaphore_signal(barrier, inc=1, device_id={"tiles": tile + 1}, device_id_type=pl.DeviceIdType.MESH)

    @pl.when(wrap_down)
    def _():
        pl.semaphore_signal(barrier, inc=1, device_id={"tiles": tile - 1}, device_id_type=pl.DeviceIdType.MESH)

    loads[0].wait()
    cut(u_ref, pieces, nu, 0, span)
    loads[1].wait()
    cut(a_ref, pieces, na, nu, span)
    for load in loads[2:]:
        load.wait()
    pack(c_ref, held, me)
    index_v[me] = jnp.zeros((1, 128), jnp.int32)
    index_v[me, :, pl.ds(0, slots)] = sb_ref[...]
    index_v[me, :, pl.ds(slots, slots)] = ei_ref[...]

    @pl.when(jnp.logical_not(has_down))
    def _():
        from_down[...] = jnp.zeros(from_down.shape, F32)

    @pl.when(jnp.logical_not(has_up))
    def _():
        from_up[...] = jnp.zeros(from_up.shape, F32)

    @pl.when(jnp.logical_not(has_last))
    def _():
        from_last[...] = jnp.zeros(from_last.shape, F32)

    @pl.when(jnp.logical_not(has_next))
    def _():
        from_next[...] = jnp.zeros(from_next.shape, F32)

    pl.semaphore_wait(barrier, 15 + row + wrap_up.astype(jnp.int32) + wrap_down.astype(jnp.int32))

    own = pltpu.make_async_copy(pieces.at[me], got.at[me], own_sem)
    own.start()
    def share(i, which, modes, to):
        return remote(held.at[which], held.at[which], c_send.at[i], c_recv.at[which], modes=modes, tiles=to)

    def quarter(i, which, q, modes, to):
        place = held.at[which, pl.ds(pl.multiple_of(nu * q, nu), nu)]
        return remote(place, place, s_send.at[i], s_recv.at[which, q], modes=modes, tiles=to)

    partner = block(0, 0, 1)
    for i, dy in enumerate((1, 3, 2)):
        quarter(i, me, x, block(0, dy, 0), tile).start()
    share(0, me, block(1, 0, 0), opposite).start()
    share(1, me, partner, tile).start()
    sends = [remote(index_v.at[me], index_v.at[me], i_send.at[i], i_recv.at[me], modes=block(*o))
             for i, o in enumerate(offsets)]
    sends += [remote(pieces.at[block(*o)], got.at[me], p_send.at[i], p_recv.at[me], modes=block(*o))
              for i, o in enumerate(offsets)]
    for copy in sends:
        copy.start()
    for n, dy in enumerate((1, 3, 2)):
        which = block(0, dy, 0)
        quarter(0, which, x, which, tile).wait_recv()
        for i, to in enumerate(beside):
            quarter(3 + 3 * n + i, which, x, me, to).start()
    def upward(g):
        return remote(up_out.at[g], from_down.at[g], m_send.at[g], m_recv.at[g], tiles=tile + 1)

    def downward(g):
        return remote(down_out.at[g], from_up.at[g], q_send.at[g], q_recv.at[g], tiles=tile - 1)

    def onward(g):
        return remote(next_out.at[g], from_last.at[g], n_send.at[g], n_recv.at[g], modes=me + 1)

    def backward(g):
        return remote(last_out.at[g], from_next.at[g], l_send.at[g], l_recv.at[g], modes=me - 1)

    lane = lanes((8, 128))
    low, zz = lane < 64, lane % 8
    own.wait()

    def pair_of(i):
        r = i % 4
        return block(i // 4, r + (r // 2) * (1 - 2 * (r % 2)), 0) // 2

    def arrived(source):
        remote(pieces.at[0], got.at[source], p_send.at[0], p_recv.at[source], modes=source).wait_recv()

    def arrive(i, carry):
        g = pair_of(i)

        @pl.when(i == 0)
        def _():
            arrived(partner)

        @pl.when(i > 0)
        def _():
            arrived(2 * g)
            arrived(2 * g + 1)

        for m in range(span // 8):
            first = pl.ds(8 * m, 8)
            second = pl.ds(span + 8 * m, 8)
            e0, e1, o0, o1 = got[2 * g, first], got[2 * g, second], got[2 * g + 1, first], got[2 * g + 1, second]
            up_out[g, first] = jnp.where(low, kroll(e1, 64), o1)
            down_out[g, first] = jnp.where(low, e0, kroll(o0, 64))
            rim = jnp.where(zz == 2, kroll(o0, 123), kroll(o1, 124))
            next_out[g, first] = jnp.where(zz == 0, kroll(e0, 121), jnp.where(zz == 1, kroll(e1, 122), rim))
            rim = jnp.where(zz == 5, kroll(o0, 5), kroll(o1, 4))
            last_out[g, first] = jnp.where(zz == 7, kroll(e0, 7), jnp.where(zz == 6, kroll(e1, 6), rim))

        @pl.when(has_up)
        def _():
            upward(g).start()

        @pl.when(has_down)
        def _():
            downward(g).start()

        @pl.when(has_next)
        def _():
            onward(g).start()

        @pl.when(has_last)
        def _():
            backward(g).start()

        for odd in range(2):
            j = 2 * g + odd
            for m in range(nu // 8):
                place = pl.ds(8 * m, 8)
                for f, value in inner_faces(difference, got[j, place], got[j, pl.ds(span + 8 * m, 8)]):
                    delta[j, f, place] = value
            place = pl.ds(pl.multiple_of(8 * j, 8), 8)
            for f, value in inner_faces(mean, got[j, pl.ds(nu, 8)], got[j, pl.ds(span + nu, 8)]):
                faces[f, place] = value
        return carry

    lax.fori_loop(0, 8, arrive, 0)
    for n, dy in enumerate((2, 1, 3)):
        which = block(0, dy, 0)
        for to in beside:
            quarter(0, which, lax.rem(to, row), me, to).wait_recv()
        share(2 + n, which, block(1, 0, 0), opposite).start()
        share(5 + n, which, partner, tile).start()

    for o in offsets:
        source = block(*o)
        remote(index_v.at[source], index_v.at[source], i_send.at[0], i_recv.at[source], modes=source).wait_recv()
    indices = pltpu.make_async_copy(index_v, index_s, own_sem)
    indices.start()

    def prepare(i, carry):
        g = pair_of(i)

        @pl.when(has_up)
        def _():
            remote(down_out.at[g], from_up.at[g], q_send.at[g], q_recv.at[g], tiles=tile + 1).wait_recv()

        @pl.when(has_down)
        def _():
            remote(up_out.at[g], from_down.at[g], m_send.at[g], m_recv.at[g], tiles=tile - 1).wait_recv()

        @pl.when(has_last)
        def _():
            remote(next_out.at[g], from_last.at[g], n_send.at[g], n_recv.at[g], modes=me - 1).wait_recv()

        @pl.when(has_next)
        def _():
            remote(last_out.at[g], from_next.at[g], l_send.at[g], l_recv.at[g], modes=me + 1).wait_recv()

        for odd in range(2):
            j = 2 * g + odd

            def tiles_of(first):
                place = pl.ds(first, 8)
                minus, plus = from_down[g, place], from_up[g, place]
                minus, plus = (kroll(minus, 64), plus) if odd else (minus, kroll(plus, 64))
                below, above = from_last[g, place], from_next[g, place]
                below = [kroll(below, 128 - n) if n else below for n in (2 * odd, 2 * odd + 1)]
                above = [kroll(above, n) if n else above for n in (2 * odd, 2 * odd + 1)]
                return got[j, place], got[j, pl.ds(span + first, 8)], below, above, minus, plus

            for m in range(nu // 8):
                for f, value in outer_faces(difference, *tiles_of(8 * m)):
                    delta[j, f, pl.ds(8 * m, 8)] = value
            place = pl.ds(pl.multiple_of(8 * j, 8), 8)
            for f, value in outer_faces(mean, *tiles_of(nu)):
                faces[f, place] = value
        return carry

    lax.fori_loop(0, 8, prepare, 0)
    indices.wait()

    def build(b, c, buffer):
        for s in range(8):
            slot = c * 8 + s
            j = index_s[b, 0, slot]
            k = index_s[b, 0, slots + slot]
            for t in range(2):
                coefficient = [faces[2 * f + t, pl.ds(k, 8, stride=0)] for f in range(6)]
                for m in range(nu // 16):
                    pair = []
                    for h in range(2):
                        rows = pl.ds(16 * m + 8 * h, 8)
                        w = coefficient[0] * delta[j, t, rows]
                        for f in range(1, 6):
                            w = w + coefficient[f] * delta[j, 2 * f + t, rows]
                        pair.append(w)
                    for h in range(2):
                        mixed[buffer, pl.ds(nu * s + 16 * m + 8 * h, 8), pl.ds(128 * t, 128)] = pair[h]

    def product(b, c, buffer):
        coupling = held[b, pl.ds(nu * c, nu)]
        high = coupling.astype(BF16)
        small = (coupling - high.astype(F32)).astype(BF16)
        w = mixed[buffer]
        w_high = w.astype(BF16)
        w_small = (w - w_high.astype(F32)).astype(BF16)
        both = jnp.dot(jnp.concatenate([high, small], axis=0), w_high, preferred_element_type=F32)
        return (both[:nu] + both[nu:]) + jnp.dot(high, w_small, preferred_element_type=F32)

    def number(k):
        k = (k + 1) % 8
        r = k % 4
        dy = r + (r // 2) * (1 - 2 * (r % 2))
        return k // 4, (dy + (k // 4) * (6 - 2 * dy)) % 4

    def landed(which):
        share(0, which, partner, tile).wait_recv()

    def deliver(i, b):
        return remote(part.at[b], back.at[me], o_send.at[i], o_recv.at[me], modes=b)

    def advance(k, carry):
        dz, dy = number(k)
        ahead = block(*number(k + 1), 0)
        own_block, other_block = block(dz, dy, 0), block(dz, dy, 1)

        @pl.when(k > 0)
        def _():
            last = number(k + 7)
            deliver(2 * k - 2, block(*last, 0)).start()
            deliver(2 * k - 1, block(*last, 1)).start()

        @pl.when((k > 1) & (k < 6))
        def _():
            landed(ahead)
            share(6 + k, ahead, partner, tile).start()

        landed(other_block)
        totals = []
        for h, b in enumerate((own_block, other_block)):
            total = None
            for c in range(slots // 8):
                build(b, c, c % 2)
                term = product(b, c, c % 2)
                total = term if total is None else total + term
            totals.append(total)
            for t in range(2):
                part[b, t] = total[:, 128 * t:128 * (t + 1)]

        @pl.when(k == 7)
        def _():
            for t in range(2):
                back[me, t] = totals[0][:, 128 * t:128 * (t + 1)]

        return carry

    lax.fori_loop(0, 8, advance, 0)
    deliver(14, partner).start()

    for dz in range(2):
        for o in offsets:
            if o[0] == dz:
                remote(part.at[0], back.at[block(*o)], o_send.at[0], o_recv.at[block(*o)], modes=block(*o)).wait_recv()
        base = 8 * lax.rem(z + dz, 2)

        def gather(m, carry):
            place = pl.ds(pl.multiple_of(8 * m, 8), 8)
            for t in range(2):
                rows = [back[base + p, t, place] for p in range(8)]
                for p, value in enumerate(transpose_blocks(rows, (1, 2, 4))):
                    back[base + p, t, place] = value
            return carry

        lax.fori_loop(0, nu // 8, gather, 0)

    def restore(m, carry):
        place = pl.ds(pl.multiple_of(8 * m, 8), 8)
        for t in range(2):
            rows = [back[p, t, place] for p in range(16)]
            for i, value in enumerate(transpose_blocks(rows, (8,))):
                out_ref[pl.ds(256 * m + 16 * t + i, 8, stride=32), :] = value
        return carry

    lax.fori_loop(0, nu // 8, restore, 0, unroll=2)
    for copy in sends:
        copy.wait_send()
    for i in range(12):
        share(i, me, partner, tile).wait_send()
        quarter(i, me, x, partner, tile).wait_send()
    for i in range(15):
        deliver(i, partner).wait_send()
    for g in range(8):
        @pl.when(has_up)
        def _():
            upward(g).wait_send()

        @pl.when(has_down)
        def _():
            downward(g).wait_send()

        @pl.when(has_next)
        def _():
            onward(g).wait_send()

        @pl.when(has_last)
        def _():
            backward(g).wait_send()


def on_device(solution_modes, coefficient_modes, coupling, source_block, expansion_index):
    nu, na = solution_modes.shape[0], coefficient_modes.shape[0]
    span, slots = nu + na, source_block.shape[1]
    rows = 2 * span
    vmem = pl.BlockSpec(memory_space=pltpu.VMEM)
    hbm = pl.BlockSpec(memory_space=pltpu.HBM)
    dma = pltpu.SemaphoreType.DMA
    out = pl.pallas_call(
        kernel,
        out_shape=jax.ShapeDtypeStruct((nu * 32, 128), F32),
        in_specs=[hbm] * 5,
        out_specs=vmem,
        scratch_shapes=[
            pltpu.VMEM((nu * 32, 128), F32), pltpu.VMEM((na * 32, 128), F32), pltpu.VMEM((slots, nu, nu), F32),
            pltpu.VMEM((1, slots), jnp.int32), pltpu.VMEM((1, slots), jnp.int32),
            pltpu.VMEM((16, rows, 128), F32), pltpu.VMEM((16, rows, 128), F32),
            *[pltpu.VMEM((8, span, 128), F32)] * 8,
            pltpu.VMEM((16, slots // 8 * nu, 256), F32),
            pltpu.VMEM((16, 2, nu, 128), F32), pltpu.VMEM((16, 2, nu, 128), F32),
            pltpu.VMEM((16, 12, nu, 128), F32), pltpu.VMEM((12, 16 * na + 8, 128), F32),
            pltpu.VMEM((2, 8 * nu, 256), F32),
            pltpu.VMEM((16, 1, 128), jnp.int32), pltpu.SMEM((16, 1, 128), jnp.int32),
            dma((5,)), dma((15,)), dma((16,)), *[dma((8,))] * 8,
            dma((12,)), dma((16,)), dma((15,)), dma((16,)), dma((15,)), dma((16,)), dma((12,)), dma((16, 4)), dma,
        ],
        compiler_params=pltpu.CompilerParams(collective_id=0, has_side_effects=True, vmem_limit_bytes=24 << 20),
        name="galerkin",
    )(*(pltpu.with_memory_space_constraint(v, pltpu.HBM) for v in (
        solution_modes.reshape(-1, 128), coefficient_modes.reshape(-1, 128), coupling[0],
        source_block, expansion_index)))
    return out.reshape(solution_modes.shape)


def solution(mesh):
    placed = (
        P("modes", "tiles", None, None),
        P("modes", "tiles", None, None),
        P("modes", None, None, None),
        P("modes", None),
        P("modes", None),
    )
    return jax.shard_map(
        on_device,
        mesh=mesh,
        in_specs=placed,
        out_specs=P("modes", "tiles", None, None),
        check_vma=False,
    )
```

```python
import functools

import jax
import jax.numpy as jnp
from jax import lax
from jax.experimental import pallas as pl
from jax.experimental.pallas import tpu as pltpu
from jax.sharding import PartitionSpec as P

F32, BF16 = jnp.float32, jnp.bfloat16


def lanes(shape):
    return lax.broadcasted_iota(jnp.int32, shape, len(shape) - 1)


def difference(own, other):
    return own - other


def mean(own, other):
    return 0.5 * (own + other)


def kroll(value, shift):
    return pltpu.roll(value, shift, value.ndim - 1)


def transpose_blocks(rows):
    lane = lanes(rows[0].shape)
    for d in (1, 2, 4, 8):
        keep = (lane // 8) & d == 0
        fresh = list(rows)
        for i in range(16):
            if not i & d:
                fresh[i] = jnp.where(keep, rows[i], kroll(rows[i + d], 8 * d))
                fresh[i + d] = jnp.where(keep, kroll(rows[i], 128 - 8 * d), rows[i + d])
        rows = fresh
    return rows


def remote(src, dst, send, recv, **where):
    return pltpu.make_async_remote_copy(
        src_ref=src, dst_ref=dst, send_sem=send, recv_sem=recv,
        device_id=where, device_id_type=pl.DeviceIdType.MESH)


def greet(others):
    barrier = pltpu.get_barrier_semaphore()
    for where in others:
        pl.semaphore_signal(barrier, inc=1, device_id=where, device_id_type=pl.DeviceIdType.MESH)
    return barrier


def face_tiles(comb, x0, x1, below, above, r_minus, r_plus):
    lane = lanes(x0.shape)
    zz, yy, low = lane % 8, (lane // 8) % 8, lane < 64
    zero = jnp.zeros_like(x0)
    r0, r1 = kroll(x0, 64), kroll(x1, 64)
    yield comb(x0, jnp.where(low, r0, r1))
    yield comb(x1, jnp.where(low, r1, r_plus))
    yield comb(x0, jnp.where(low, r_minus, r0))
    yield comb(x1, jnp.where(low, r0, r1))
    for x in (x0, x1):
        yield comb(x, jnp.where(yy < 7, kroll(x, 120), zero))
    for x in (x0, x1):
        yield comb(x, jnp.where(yy > 0, kroll(x, 8), zero))
    for x, rim in zip((x0, x1), above):
        yield comb(x, jnp.where(zz < 7, kroll(x, 127), rim))
    for x, rim in zip((x0, x1), below):
        yield comb(x, jnp.where(zz > 0, kroll(x, 1), rim))


def cut(value_ref, pieces, count, first, span):
    def one(m, carry):
        for t in range(2):
            place = pl.ds(pl.multiple_of(span * t + first + 8 * m, 8), 8)
            rows = [value_ref[pl.ds(256 * m + 16 * t + i, 8, stride=32), :] for i in range(16)]
            for p, value in enumerate(transpose_blocks(rows)):
                pieces[p, place] = value
        return carry

    lax.fori_loop(0, count // 8, one, 0, unroll=2 if count > 8 else 1)


def pack(c_ref, held, me):
    n = c_ref.shape[1]
    for q in range(4):
        for h in range(2):
            for m in range(n // 8):
                parts = [c_ref[8 * q + 4 * h + l, pl.ds(8 * m, 8), :] for l in range(4)]
                held[me, pl.ds(n * q + 8 * m, 8), pl.ds(128 * h, 128)] = jnp.concatenate(parts, axis=1)


def kernel(u_hbm, a_hbm, c_hbm, sb_hbm, ei_hbm, out_ref,
           u_ref, a_ref, c_ref, sb_ref, ei_ref, pieces, got, up_out, down_out, from_down, from_up,
           next_out, last_out, from_last, from_next, held, part, back,
           delta, faces, mixed, index_v, index_s,
           in_sem, p_send, p_recv, m_send, m_recv, q_send, q_recv,
           n_send, n_recv, l_send, l_recv, c_send, c_recv, o_send, o_recv, i_send, i_recv, s_send, s_recv, own_sem):
    me, tile = lax.axis_index("modes"), lax.axis_index("tiles")
    tiles = lax.axis_size("tiles")
    has_up, has_down = tile < tiles - 1, tile > 0
    has_next, has_last = me < 15, me > 0
    z, y, core = me // 8, lax.rem(me // 2, 4), lax.rem(me, 2)
    nu, na = u_ref.shape[0] // 32, a_ref.shape[0] // 32
    span = nu + na
    slots = c_ref.shape[0]

    def block(dz, dy, dc):
        return lax.rem(z + dz, 2) * 8 + lax.rem(y + dy, 4) * 2 + lax.rem(core + dc, 2)

    loads = [pltpu.make_async_copy(s, d, in_sem.at[i])
             for i, (s, d) in enumerate(((u_hbm, u_ref), (a_hbm, a_ref), (c_hbm, c_ref), (sb_hbm, sb_ref), (ei_hbm, ei_ref)))]
    for load in loads:
        load.start()
    row = tiles // 2
    opposite = lax.rem(tile + row, tiles)
    x = lax.rem(tile, row)
    beside = [tile - x + lax.rem(x + d, row) for d in range(1, row)]
    chips = ((0, 0), (0, 1), (0, 3), (1, 0), (0, 2), (1, 1), (1, 3), (1, 2))
    offsets = [(dz, dy, dc) for dz, dy in chips for dc in range(2)][1:]
    barrier = greet([{"modes": block(*o)} for o in offsets] + [{"modes": block(1, 0, 0), "tiles": opposite}]
                    + [{"tiles": t} for t in beside])
    wrap_up, wrap_down = has_up & (x == row - 1), has_down & (x == 0)

    @pl.when(wrap_up)
    def _():
        pl.semaphore_signal(barrier, inc=1, device_id={"tiles": tile + 1}, device_id_type=pl.DeviceIdType.MESH)

    @pl.when(wrap_down)
    def _():
        pl.semaphore_signal(barrier, inc=1, device_id={"tiles": tile - 1}, device_id_type=pl.DeviceIdType.MESH)

    loads[0].wait()
    cut(u_ref, pieces, nu, 0, span)
    loads[1].wait()
    cut(a_ref, pieces, na, nu, span)
    for load in loads[2:]:
        load.wait()
    pack(c_ref, held, me)
    index_v[me] = jnp.zeros((1, 128), jnp.int32)
    index_v[me, :, pl.ds(0, slots)] = sb_ref[...]
    index_v[me, :, pl.ds(slots, slots)] = ei_ref[...]

    @pl.when(jnp.logical_not(has_down))
    def _():
        from_down[...] = jnp.zeros(from_down.shape, F32)

    @pl.when(jnp.logical_not(has_up))
    def _():
        from_up[...] = jnp.zeros(from_up.shape, F32)

    @pl.when(jnp.logical_not(has_last))
    def _():
        from_last[...] = jnp.zeros(from_last.shape, F32)

    @pl.when(jnp.logical_not(has_next))
    def _():
        from_next[...] = jnp.zeros(from_next.shape, F32)

    pl.semaphore_wait(barrier, 15 + row + wrap_up.astype(jnp.int32) + wrap_down.astype(jnp.int32))

    own = pltpu.make_async_copy(pieces.at[me], got.at[me], own_sem)
    own.start()
    def share(i, which, modes, to):
        return remote(held.at[which], held.at[which], c_send.at[i], c_recv.at[which], modes=modes, tiles=to)

    def quarter(i, which, q, modes, to):
        place = held.at[which, pl.ds(pl.multiple_of(nu * q, nu), nu)]
        return remote(place, place, s_send.at[i], s_recv.at[which, q], modes=modes, tiles=to)

    partner = block(0, 0, 1)
    for i, dy in enumerate((1, 3, 2)):
        quarter(i, me, x, block(0, dy, 0), tile).start()
    share(0, me, block(1, 0, 0), opposite).start()
    share(1, me, partner, tile).start()
    sends = [remote(index_v.at[me], index_v.at[me], i_send.at[i], i_recv.at[me], modes=block(*o))
             for i, o in enumerate(offsets)]
    sends += [remote(pieces.at[block(*o)], got.at[me], p_send.at[i], p_recv.at[me], modes=block(*o))
              for i, o in enumerate(offsets)]
    for copy in sends:
        copy.start()
    for n, dy in enumerate((1, 3, 2)):
        which = block(0, dy, 0)
        quarter(0, which, x, which, tile).wait_recv()
        for i, to in enumerate(beside):
            quarter(3 + 3 * n + i, which, x, me, to).start()
    def upward(g):
        return remote(up_out.at[g], from_down.at[g], m_send.at[g], m_recv.at[g], tiles=tile + 1)

    def downward(g):
        return remote(down_out.at[g], from_up.at[g], q_send.at[g], q_recv.at[g], tiles=tile - 1)

    def onward(g):
        return remote(next_out.at[g], from_last.at[g], n_send.at[g], n_recv.at[g], modes=me + 1)

    def backward(g):
        return remote(last_out.at[g], from_next.at[g], l_send.at[g], l_recv.at[g], modes=me - 1)

    lane = lanes((8, 128))
    low, zz = lane < 64, lane % 8
    own.wait()
    for dz, dy in chips:
        for dc in range(2):
            if (dz, dy, dc) != (0, 0, 0):
                source = block(dz, dy, dc)
                remote(pieces.at[1], got.at[source], p_send.at[0], p_recv.at[source], modes=source).wait_recv()
        g = block(dz, dy, 0) // 2
        for m in range(span // 8):
            first = pl.ds(8 * m, 8)
            second = pl.ds(span + 8 * m, 8)
            e0, e1, o0, o1 = got[2 * g, first], got[2 * g, second], got[2 * g + 1, first], got[2 * g + 1, second]
            up_out[g, first] = jnp.where(low, kroll(e1, 64), o1)
            down_out[g, first] = jnp.where(low, e0, kroll(o0, 64))
            rim = jnp.where(zz == 2, kroll(o0, 123), kroll(o1, 124))
            next_out[g, first] = jnp.where(zz == 0, kroll(e0, 121), jnp.where(zz == 1, kroll(e1, 122), rim))
            rim = jnp.where(zz == 5, kroll(o0, 5), kroll(o1, 4))
            last_out[g, first] = jnp.where(zz == 7, kroll(e0, 7), jnp.where(zz == 6, kroll(e1, 6), rim))

        @pl.when(has_up)
        def _():
            upward(g).start()

        @pl.when(has_down)
        def _():
            downward(g).start()

        @pl.when(has_next)
        def _():
            onward(g).start()

        @pl.when(has_last)
        def _():
            backward(g).start()

    for n, dy in enumerate((1, 3, 2)):
        which = block(0, dy, 0)
        for to in beside:
            quarter(0, which, lax.rem(to, row), me, to).wait_recv()
        share(2 + n, which, block(1, 0, 0), tile if dy == 3 else opposite).start()
        share(5 + n, which, partner, tile).start()

    for o in offsets:
        source = block(*o)
        remote(index_v.at[source], index_v.at[source], i_send.at[0], i_recv.at[source], modes=source).wait_recv()
    indices = pltpu.make_async_copy(index_v, index_s, own_sem)
    indices.start()

    def prepare(i, carry):
        dz, r = i // 4, i % 4
        g = block(dz, r + (r // 2) * (1 - 2 * (r % 2)), 0) // 2

        @pl.when(has_up)
        def _():
            remote(down_out.at[g], from_up.at[g], q_send.at[g], q_recv.at[g], tiles=tile + 1).wait_recv()

        @pl.when(has_down)
        def _():
            remote(up_out.at[g], from_down.at[g], m_send.at[g], m_recv.at[g], tiles=tile - 1).wait_recv()

        @pl.when(has_last)
        def _():
            remote(next_out.at[g], from_last.at[g], n_send.at[g], n_recv.at[g], modes=me - 1).wait_recv()

        @pl.when(has_next)
        def _():
            remote(last_out.at[g], from_next.at[g], l_send.at[g], l_recv.at[g], modes=me + 1).wait_recv()

        for odd in range(2):
            j = 2 * g + odd

            def tiles_of(first):
                place = pl.ds(first, 8)
                minus, plus = from_down[g, place], from_up[g, place]
                minus, plus = (kroll(minus, 64), plus) if odd else (minus, kroll(plus, 64))
                below, above = from_last[g, place], from_next[g, place]
                below = [kroll(below, 128 - n) if n else below for n in (2 * odd, 2 * odd + 1)]
                above = [kroll(above, n) if n else above for n in (2 * odd, 2 * odd + 1)]
                return got[j, place], got[j, pl.ds(span + first, 8)], below, above, minus, plus

            for m in range(nu // 8):
                for f, value in enumerate(face_tiles(difference, *tiles_of(8 * m))):
                    delta[j, f, pl.ds(8 * m, 8)] = value
            place = pl.ds(pl.multiple_of(8 * j, 8), 8)
            for f, value in enumerate(face_tiles(mean, *tiles_of(nu))):
                faces[f, place] = value
        return carry

    lax.fori_loop(0, 8, prepare, 0)
    indices.wait()

    def build(b, c, buffer):
        for s in range(8):
            slot = c * 8 + s
            j = index_s[b, 0, slot]
            k = index_s[b, 0, slots + slot]
            for t in range(2):
                coefficient = [faces[2 * f + t, pl.ds(k, 8, stride=0)] for f in range(6)]
                for m in range(nu // 16):
                    pair = []
                    for h in range(2):
                        rows = pl.ds(16 * m + 8 * h, 8)
                        w = coefficient[0] * delta[j, t, rows]
                        for f in range(1, 6):
                            w = w + coefficient[f] * delta[j, 2 * f + t, rows]
                        pair.append(w)
                    for h in range(2):
                        mixed[buffer, pl.ds(nu * s + 16 * m + 8 * h, 8), pl.ds(128 * t, 128)] = pair[h]

    def product(b, c, buffer):
        coupling = held[b, pl.ds(nu * c, nu)]
        high = coupling.astype(BF16)
        small = (coupling - high.astype(F32)).astype(BF16)
        w = mixed[buffer]
        w_high = w.astype(BF16)
        w_small = (w - w_high.astype(F32)).astype(BF16)
        both = jnp.dot(jnp.concatenate([high, small], axis=0), w_high, preferred_element_type=F32)
        return (both[:nu] + both[nu:]) + jnp.dot(high, w_small, preferred_element_type=F32)

    def number(k):
        k = (k + 1) % 8
        r = k % 4
        return k // 4, r + (r // 2) * (1 - 2 * (r % 2))

    def landed(which):
        share(0, which, partner, tile).wait_recv()

    def deliver(i, b):
        return remote(part.at[b], back.at[me], o_send.at[i], o_recv.at[me], modes=b)

    def advance(k, carry):
        dz, dy = number(k)
        ahead = block(*number(k + 1), 0)
        own_block, other_block = block(dz, dy, 0), block(dz, dy, 1)

        @pl.when(k > 0)
        def _():
            last = number(k + 7)
            deliver(2 * k - 2, block(*last, 0)).start()
            deliver(2 * k - 1, block(*last, 1)).start()

        @pl.when((k > 1) & (k < 6))
        def _():
            landed(ahead)
            share(6 + k, ahead, partner, tile).start()

        landed(other_block)
        totals = []
        for h, b in enumerate((own_block, other_block)):
            total = None
            for c in range(slots // 8):
                build(b, c, c % 2)
                term = product(b, c, c % 2)
                total = term if total is None else total + term
            totals.append(total)
            for t in range(2):
                part[b, t] = total[:, 128 * t:128 * (t + 1)]

        @pl.when(k == 7)
        def _():
            for t in range(2):
                back[me, t] = totals[0][:, 128 * t:128 * (t + 1)]

        return carry

    lax.fori_loop(0, 8, advance, 0)
    deliver(14, partner).start()

    for dz, dy, dc in offsets:
        source = block(dz, dy, dc)
        remote(part.at[0], back.at[source], o_send.at[0], o_recv.at[source], modes=source).wait_recv()

    def restore(m, carry):
        place = pl.ds(pl.multiple_of(8 * m, 8), 8)
        for t in range(2):
            rows = [back[p, t, place] for p in range(16)]
            for i, value in enumerate(transpose_blocks(rows)):
                out_ref[pl.ds(256 * m + 16 * t + i, 8, stride=32), :] = value
        return carry

    lax.fori_loop(0, nu // 8, restore, 0, unroll=2)
    for copy in sends:
        copy.wait_send()
    for i in range(12):
        share(i, me, partner, tile).wait_send()
        quarter(i, me, x, partner, tile).wait_send()
    for i in range(15):
        deliver(i, partner).wait_send()
    for g in range(8):
        @pl.when(has_up)
        def _():
            upward(g).wait_send()

        @pl.when(has_down)
        def _():
            downward(g).wait_send()

        @pl.when(has_next)
        def _():
            onward(g).wait_send()

        @pl.when(has_last)
        def _():
            backward(g).wait_send()


def on_device(solution_modes, coefficient_modes, coupling, source_block, expansion_index):
    nu, na = solution_modes.shape[0], coefficient_modes.shape[0]
    span, slots = nu + na, source_block.shape[1]
    rows = 2 * span
    vmem = pl.BlockSpec(memory_space=pltpu.VMEM)
    hbm = pl.BlockSpec(memory_space=pltpu.HBM)
    dma = pltpu.SemaphoreType.DMA
    out = pl.pallas_call(
        kernel,
        out_shape=jax.ShapeDtypeStruct((nu * 32, 128), F32),
        in_specs=[hbm] * 5,
        out_specs=vmem,
        scratch_shapes=[
            pltpu.VMEM((nu * 32, 128), F32), pltpu.VMEM((na * 32, 128), F32), pltpu.VMEM((slots, nu, nu), F32),
            pltpu.VMEM((1, slots), jnp.int32), pltpu.VMEM((1, slots), jnp.int32),
            pltpu.VMEM((16, rows, 128), F32), pltpu.VMEM((16, rows, 128), F32),
            *[pltpu.VMEM((8, span, 128), F32)] * 8,
            pltpu.VMEM((16, slots // 8 * nu, 256), F32),
            pltpu.VMEM((16, 2, nu, 128), F32), pltpu.VMEM((16, 2, nu, 128), F32),
            pltpu.VMEM((16, 12, nu, 128), F32), pltpu.VMEM((12, 16 * na + 8, 128), F32),
            pltpu.VMEM((2, 8 * nu, 256), F32),
            pltpu.VMEM((16, 1, 128), jnp.int32), pltpu.SMEM((16, 1, 128), jnp.int32),
            dma((5,)), dma((15,)), dma((16,)), *[dma((8,))] * 8,
            dma((12,)), dma((16,)), dma((15,)), dma((16,)), dma((15,)), dma((16,)), dma((12,)), dma((16, 4)), dma,
        ],
        compiler_params=pltpu.CompilerParams(collective_id=0, has_side_effects=True, vmem_limit_bytes=24 << 20),
        name="galerkin",
    )(*(pltpu.with_memory_space_constraint(v, pltpu.HBM) for v in (
        solution_modes.reshape(-1, 128), coefficient_modes.reshape(-1, 128), coupling[0],
        source_block, expansion_index)))
    return out.reshape(solution_modes.shape)


def solution(mesh):
    placed = (
        P("modes", "tiles", None, None),
        P("modes", "tiles", None, None),
        P("modes", None, None, None),
        P("modes", None),
        P("modes", None),
    )
    return jax.shard_map(
        on_device,
        mesh=mesh,
        in_specs=placed,
        out_specs=P("modes", "tiles", None, None),
        check_vma=False,
    )
```

```python
import functools

import jax
import jax.numpy as jnp
from jax import lax
from jax.experimental import pallas as pl
from jax.experimental.pallas import tpu as pltpu
from jax.sharding import PartitionSpec as P

F32, BF16 = jnp.float32, jnp.bfloat16


def lanes(shape):
    return lax.broadcasted_iota(jnp.int32, shape, len(shape) - 1)


def difference(own, other):
    return own - other


def mean(own, other):
    return 0.5 * (own + other)


def kroll(value, shift):
    return pltpu.roll(value, shift, value.ndim - 1)


def transpose_blocks(rows):
    lane = lanes(rows[0].shape)
    for d in (1, 2, 4, 8):
        keep = (lane // 8) & d == 0
        fresh = list(rows)
        for i in range(16):
            if not i & d:
                fresh[i] = jnp.where(keep, rows[i], kroll(rows[i + d], 8 * d))
                fresh[i + d] = jnp.where(keep, kroll(rows[i], 128 - 8 * d), rows[i + d])
        rows = fresh
    return rows


def remote(src, dst, send, recv, **where):
    return pltpu.make_async_remote_copy(
        src_ref=src, dst_ref=dst, send_sem=send, recv_sem=recv,
        device_id=where, device_id_type=pl.DeviceIdType.MESH)


def greet(others):
    barrier = pltpu.get_barrier_semaphore()
    for where in others:
        pl.semaphore_signal(barrier, inc=1, device_id=where, device_id_type=pl.DeviceIdType.MESH)
    return barrier


def face_tiles(comb, x0, x1, below, above, r_minus, r_plus):
    lane = lanes(x0.shape)
    zz, yy, low = lane % 8, (lane // 8) % 8, lane < 64
    zero = jnp.zeros_like(x0)
    r0, r1 = kroll(x0, 64), kroll(x1, 64)
    yield comb(x0, jnp.where(low, r0, r1))
    yield comb(x1, jnp.where(low, r1, r_plus))
    yield comb(x0, jnp.where(low, r_minus, r0))
    yield comb(x1, jnp.where(low, r0, r1))
    for x in (x0, x1):
        yield comb(x, jnp.where(yy < 7, kroll(x, 120), zero))
    for x in (x0, x1):
        yield comb(x, jnp.where(yy > 0, kroll(x, 8), zero))
    for x, rim in zip((x0, x1), above):
        yield comb(x, jnp.where(zz < 7, kroll(x, 127), rim))
    for x, rim in zip((x0, x1), below):
        yield comb(x, jnp.where(zz > 0, kroll(x, 1), rim))


def cut(value_ref, pieces, count, first, span):
    def one(m, carry):
        for t in range(2):
            place = pl.ds(pl.multiple_of(span * t + first + 8 * m, 8), 8)
            rows = [value_ref[pl.ds(256 * m + 16 * t + i, 8, stride=32), :] for i in range(16)]
            for p, value in enumerate(transpose_blocks(rows)):
                pieces[p, place] = value
        return carry

    lax.fori_loop(0, count // 8, one, 0, unroll=2 if count > 8 else 1)


def pack(c_ref, held, me):
    n = c_ref.shape[1]
    for q in range(4):
        for h in range(2):
            for m in range(n // 8):
                parts = [c_ref[8 * q + 4 * h + l, pl.ds(8 * m, 8), :] for l in range(4)]
                held[me, pl.ds(n * q + 8 * m, 8), pl.ds(128 * h, 128)] = jnp.concatenate(parts, axis=1)


def kernel(u_hbm, a_hbm, c_hbm, sb_hbm, ei_hbm, out_ref,
           u_ref, a_ref, c_ref, sb_ref, ei_ref, pieces, got, up_out, down_out, from_down, from_up,
           next_out, last_out, from_last, from_next, held, part, back,
           delta, faces, mixed, index_v, index_s,
           in_sem, p_send, p_recv, m_send, m_recv, q_send, q_recv,
           n_send, n_recv, l_send, l_recv, c_send, c_recv, o_send, o_recv, i_send, i_recv, s_send, s_recv, own_sem):
    me, tile = lax.axis_index("modes"), lax.axis_index("tiles")
    tiles = lax.axis_size("tiles")
    has_up, has_down = tile < tiles - 1, tile > 0
    has_next, has_last = me < 15, me > 0
    z, y, core = me // 8, lax.rem(me // 2, 4), lax.rem(me, 2)
    nu, na = u_ref.shape[0] // 32, a_ref.shape[0] // 32
    span = nu + na
    slots = c_ref.shape[0]

    def block(dz, dy, dc):
        return lax.rem(z + dz, 2) * 8 + lax.rem(y + dy, 4) * 2 + lax.rem(core + dc, 2)

    loads = [pltpu.make_async_copy(s, d, in_sem.at[i])
             for i, (s, d) in enumerate(((u_hbm, u_ref), (a_hbm, a_ref), (c_hbm, c_ref), (sb_hbm, sb_ref), (ei_hbm, ei_ref)))]
    for load in loads:
        load.start()
    row = tiles // 2
    opposite = lax.rem(tile + row, tiles)
    x = lax.rem(tile, row)
    beside = [tile - x + lax.rem(x + d, row) for d in range(1, row)]
    chips = ((0, 0), (0, 1), (0, 3), (1, 0), (0, 2), (1, 1), (1, 3), (1, 2))
    offsets = [(dz, dy, dc) for dz, dy in chips for dc in range(2)][1:]
    barrier = greet([{"modes": block(*o)} for o in offsets] + [{"modes": block(1, 0, 0), "tiles": opposite}]
                    + [{"tiles": t} for t in beside])
    wrap_up, wrap_down = has_up & (x == row - 1), has_down & (x == 0)

    @pl.when(wrap_up)
    def _():
        pl.semaphore_signal(barrier, inc=1, device_id={"tiles": tile + 1}, device_id_type=pl.DeviceIdType.MESH)

    @pl.when(wrap_down)
    def _():
        pl.semaphore_signal(barrier, inc=1, device_id={"tiles": tile - 1}, device_id_type=pl.DeviceIdType.MESH)

    loads[0].wait()
    cut(u_ref, pieces, nu, 0, span)
    loads[1].wait()
    cut(a_ref, pieces, na, nu, span)
    for load in loads[2:]:
        load.wait()
    pack(c_ref, held, me)
    index_v[me] = jnp.zeros((1, 128), jnp.int32)
    index_v[me, :, pl.ds(0, slots)] = sb_ref[...]
    index_v[me, :, pl.ds(slots, slots)] = ei_ref[...]

    @pl.when(jnp.logical_not(has_down))
    def _():
        from_down[...] = jnp.zeros(from_down.shape, F32)

    @pl.when(jnp.logical_not(has_up))
    def _():
        from_up[...] = jnp.zeros(from_up.shape, F32)

    @pl.when(jnp.logical_not(has_last))
    def _():
        from_last[...] = jnp.zeros(from_last.shape, F32)

    @pl.when(jnp.logical_not(has_next))
    def _():
        from_next[...] = jnp.zeros(from_next.shape, F32)

    pl.semaphore_wait(barrier, 15 + row + wrap_up.astype(jnp.int32) + wrap_down.astype(jnp.int32))

    own = pltpu.make_async_copy(pieces.at[me], got.at[me], own_sem)
    own.start()
    def share(i, which, modes, to):
        return remote(held.at[which], held.at[which], c_send.at[i], c_recv.at[which], modes=modes, tiles=to)

    def quarter(i, which, q, modes, to):
        place = held.at[which, pl.ds(pl.multiple_of(nu * q, nu), nu)]
        return remote(place, place, s_send.at[i], s_recv.at[which, q], modes=modes, tiles=to)

    partner = block(0, 0, 1)
    for i, dy in enumerate((1, 3, 2)):
        quarter(i, me, x, block(0, dy, 0), tile).start()
    share(0, me, block(1, 0, 0), opposite).start()
    share(1, me, partner, tile).start()
    sends = [remote(index_v.at[me], index_v.at[me], i_send.at[i], i_recv.at[me], modes=block(*o))
             for i, o in enumerate(offsets)]
    sends += [remote(pieces.at[block(*o)], got.at[me], p_send.at[i], p_recv.at[me], modes=block(*o))
              for i, o in enumerate(offsets)]
    for copy in sends:
        copy.start()
    for n, dy in enumerate((1, 3, 2)):
        which = block(0, dy, 0)
        quarter(0, which, x, which, tile).wait_recv()
        for i, to in enumerate(beside):
            quarter(3 + 3 * n + i, which, x, me, to).start()
    def upward(g):
        return remote(up_out.at[g], from_down.at[g], m_send.at[g], m_recv.at[g], tiles=tile + 1)

    def downward(g):
        return remote(down_out.at[g], from_up.at[g], q_send.at[g], q_recv.at[g], tiles=tile - 1)

    def onward(g):
        return remote(next_out.at[g], from_last.at[g], n_send.at[g], n_recv.at[g], modes=me + 1)

    def backward(g):
        return remote(last_out.at[g], from_next.at[g], l_send.at[g], l_recv.at[g], modes=me - 1)

    lane = lanes((8, 128))
    low, zz = lane < 64, lane % 8
    own.wait()
    for dz, dy in chips:
        for dc in range(2):
            if (dz, dy, dc) != (0, 0, 0):
                source = block(dz, dy, dc)
                remote(pieces.at[1], got.at[source], p_send.at[0], p_recv.at[source], modes=source).wait_recv()
        g = block(dz, dy, 0) // 2
        for m in range(span // 8):
            first = pl.ds(8 * m, 8)
            second = pl.ds(span + 8 * m, 8)
            e0, e1, o0, o1 = got[2 * g, first], got[2 * g, second], got[2 * g + 1, first], got[2 * g + 1, second]
            up_out[g, first] = jnp.where(low, kroll(e1, 64), o1)
            down_out[g, first] = jnp.where(low, e0, kroll(o0, 64))
            rim = jnp.where(zz == 2, kroll(o0, 123), kroll(o1, 124))
            next_out[g, first] = jnp.where(zz == 0, kroll(e0, 121), jnp.where(zz == 1, kroll(e1, 122), rim))
            rim = jnp.where(zz == 5, kroll(o0, 5), kroll(o1, 4))
            last_out[g, first] = jnp.where(zz == 7, kroll(e0, 7), jnp.where(zz == 6, kroll(e1, 6), rim))

        @pl.when(has_up)
        def _():
            upward(g).start()

        @pl.when(has_down)
        def _():
            downward(g).start()

        @pl.when(has_next)
        def _():
            onward(g).start()

        @pl.when(has_last)
        def _():
            backward(g).start()

    for n, dy in enumerate((1, 3, 2)):
        which = block(0, dy, 0)
        for to in beside:
            quarter(0, which, lax.rem(to, row), me, to).wait_recv()
        share(2 + n, which, block(1, 0, 0), tile if dy == 3 else opposite).start()
        share(5 + n, which, partner, tile).start()

    for o in offsets:
        source = block(*o)
        remote(index_v.at[source], index_v.at[source], i_send.at[0], i_recv.at[source], modes=source).wait_recv()
    indices = pltpu.make_async_copy(index_v, index_s, own_sem)
    indices.start()

    def prepare(i, carry):
        dz, r = i // 4, i % 4
        g = block(dz, r + (r // 2) * (1 - 2 * (r % 2)), 0) // 2

        @pl.when(has_up)
        def _():
            remote(down_out.at[g], from_up.at[g], q_send.at[g], q_recv.at[g], tiles=tile + 1).wait_recv()

        @pl.when(has_down)
        def _():
            remote(up_out.at[g], from_down.at[g], m_send.at[g], m_recv.at[g], tiles=tile - 1).wait_recv()

        @pl.when(has_last)
        def _():
            remote(next_out.at[g], from_last.at[g], n_send.at[g], n_recv.at[g], modes=me - 1).wait_recv()

        @pl.when(has_next)
        def _():
            remote(last_out.at[g], from_next.at[g], l_send.at[g], l_recv.at[g], modes=me + 1).wait_recv()

        for odd in range(2):
            j = 2 * g + odd

            def tiles_of(first):
                place = pl.ds(first, 8)
                minus, plus = from_down[g, place], from_up[g, place]
                minus, plus = (kroll(minus, 64), plus) if odd else (minus, kroll(plus, 64))
                below, above = from_last[g, place], from_next[g, place]
                below = [kroll(below, 128 - n) if n else below for n in (2 * odd, 2 * odd + 1)]
                above = [kroll(above, n) if n else above for n in (2 * odd, 2 * odd + 1)]
                return got[j, place], got[j, pl.ds(span + first, 8)], below, above, minus, plus

            for m in range(nu // 8):
                for f, value in enumerate(face_tiles(difference, *tiles_of(8 * m))):
                    delta[j, f, pl.ds(8 * m, 8)] = value
            place = pl.ds(pl.multiple_of(8 * j, 8), 8)
            for f, value in enumerate(face_tiles(mean, *tiles_of(nu))):
                faces[f, place] = value
        return carry

    lax.fori_loop(0, 8, prepare, 0)
    indices.wait()

    def build(b, c, buffer):
        for s in range(8):
            slot = c * 8 + s
            j = index_s[b, 0, slot]
            k = index_s[b, 0, slots + slot]
            for t in range(2):
                coefficient = [faces[2 * f + t, pl.ds(k, 8, stride=0)] for f in range(6)]
                for m in range(nu // 16):
                    pair = []
                    for h in range(2):
                        rows = pl.ds(16 * m + 8 * h, 8)
                        w = coefficient[0] * delta[j, t, rows]
                        for f in range(1, 6):
                            w = w + coefficient[f] * delta[j, 2 * f + t, rows]
                        pair.append(w)
                    for h in range(2):
                        mixed[buffer, pl.ds(nu * s + 16 * m + 8 * h, 8), pl.ds(128 * t, 128)] = pair[h]

    def product(b, c, buffer):
        coupling = held[b, pl.ds(nu * c, nu)]
        high = coupling.astype(BF16)
        small = (coupling - high.astype(F32)).astype(BF16)
        w = mixed[buffer]
        w_high = w.astype(BF16)
        w_small = (w - w_high.astype(F32)).astype(BF16)
        both = jnp.dot(jnp.concatenate([high, small], axis=0), w_high, preferred_element_type=F32)
        return (both[:nu] + both[nu:]) + jnp.dot(high, w_small, preferred_element_type=F32)

    def number(k):
        k = (k + 1) % 8
        r = k % 4
        return k // 4, r + (r // 2) * (1 - 2 * (r % 2))

    def landed(which):
        share(0, which, partner, tile).wait_recv()

    def deliver(i, b):
        return remote(part.at[b], back.at[me], o_send.at[i], o_recv.at[me], modes=b)

    def advance(k, carry):
        dz, dy = number(k)
        ahead = block(*number(k + 1), 0)
        own_block, other_block = block(dz, dy, 0), block(dz, dy, 1)

        @pl.when(k > 0)
        def _():
            last = number(k + 7)
            deliver(2 * k - 2, block(*last, 0)).start()
            deliver(2 * k - 1, block(*last, 1)).start()

        @pl.when((k > 1) & (k < 6))
        def _():
            landed(ahead)
            share(6 + k, ahead, partner, tile).start()

        landed(other_block)
        totals = []
        for h, b in enumerate((own_block, other_block)):
            total = None
            for c in range(slots // 8):
                build(b, c, c % 2)
                term = product(b, c, c % 2)
                total = term if total is None else total + term
            totals.append(total)
            for t in range(2):
                part[b, t] = total[:, 128 * t:128 * (t + 1)]

        @pl.when(k == 7)
        def _():
            for t in range(2):
                back[me, t] = totals[0][:, 128 * t:128 * (t + 1)]

        return carry

    lax.fori_loop(0, 8, advance, 0)
    deliver(14, partner).start()

    for copy in sends:
        copy.wait_send()
    for i in range(12):
        share(i, me, partner, tile).wait_send()
        quarter(i, me, x, partner, tile).wait_send()

    def drained(g, carry):
        @pl.when(has_up)
        def _():
            upward(g).wait_send()

        @pl.when(has_down)
        def _():
            downward(g).wait_send()

        @pl.when(has_next)
        def _():
            onward(g).wait_send()

        @pl.when(has_last)
        def _():
            backward(g).wait_send()
        return carry

    lax.fori_loop(0, 8, drained, 0)
    for dz, dy, dc in offsets:
        source = block(dz, dy, dc)
        remote(part.at[0], back.at[source], o_send.at[0], o_recv.at[source], modes=source).wait_recv()

    def restore(m, carry):
        place = pl.ds(pl.multiple_of(8 * m, 8), 8)
        for t in range(2):
            rows = [back[p, t, place] for p in range(16)]
            for i, value in enumerate(transpose_blocks(rows)):
                out_ref[pl.ds(256 * m + 16 * t + i, 8, stride=32), :] = value
        return carry

    lax.fori_loop(0, nu // 8, restore, 0, unroll=2)
    for i in range(15):
        deliver(i, partner).wait_send()


def on_device(solution_modes, coefficient_modes, coupling, source_block, expansion_index):
    nu, na = solution_modes.shape[0], coefficient_modes.shape[0]
    span, slots = nu + na, source_block.shape[1]
    rows = 2 * span
    vmem = pl.BlockSpec(memory_space=pltpu.VMEM)
    hbm = pl.BlockSpec(memory_space=pltpu.HBM)
    dma = pltpu.SemaphoreType.DMA
    out = pl.pallas_call(
        kernel,
        out_shape=jax.ShapeDtypeStruct((nu * 32, 128), F32),
        in_specs=[hbm] * 5,
        out_specs=vmem,
        scratch_shapes=[
            pltpu.VMEM((nu * 32, 128), F32), pltpu.VMEM((na * 32, 128), F32), pltpu.VMEM((slots, nu, nu), F32),
            pltpu.VMEM((1, slots), jnp.int32), pltpu.VMEM((1, slots), jnp.int32),
            pltpu.VMEM((16, rows, 128), F32), pltpu.VMEM((16, rows, 128), F32),
            *[pltpu.VMEM((8, span, 128), F32)] * 8,
            pltpu.VMEM((16, slots // 8 * nu, 256), F32),
            pltpu.VMEM((16, 2, nu, 128), F32), pltpu.VMEM((16, 2, nu, 128), F32),
            pltpu.VMEM((16, 12, nu, 128), F32), pltpu.VMEM((12, 16 * na + 8, 128), F32),
            pltpu.VMEM((2, 8 * nu, 256), F32),
            pltpu.VMEM((16, 1, 128), jnp.int32), pltpu.SMEM((16, 1, 128), jnp.int32),
            dma((5,)), dma((15,)), dma((16,)), *[dma((8,))] * 8,
            dma((12,)), dma((16,)), dma((15,)), dma((16,)), dma((15,)), dma((16,)), dma((12,)), dma((16, 4)), dma,
        ],
        compiler_params=pltpu.CompilerParams(collective_id=0, has_side_effects=True, vmem_limit_bytes=24 << 20),
        name="galerkin",
    )(*(pltpu.with_memory_space_constraint(v, pltpu.HBM) for v in (
        solution_modes.reshape(-1, 128), coefficient_modes.reshape(-1, 128), coupling[0],
        source_block, expansion_index)))
    return out.reshape(solution_modes.shape)


def solution(mesh):
    placed = (
        P("modes", "tiles", None, None),
        P("modes", "tiles", None, None),
        P("modes", None, None, None),
        P("modes", None),
        P("modes", None),
    )
    return jax.shard_map(
        on_device,
        mesh=mesh,
        in_specs=placed,
        out_specs=P("modes", "tiles", None, None),
        check_vma=False,
    )
```
